128 devices in a mesh: ax: 8 (over x, core), az: 16 (over z, y).
Axes of the slice: x: 4, y: 4, z: 4, core: 2. Of those that a mesh axis runs over, the one named last changes fastest.
Arguments:
- particles: float32 [32, 256, 128, 128], P('ax', 'az'), may hold values from -8 to 8, as said below
- counts: int32 [32, 256], P('ax', 'az'), may hold values from 48 to 128
- pair_codes: int32 [32, 256, 6], P('ax', 'az'), may hold values from 0 to 8, as said below
- contact: int32 [32, 256], P('ax', 'az'), may hold values from 0 to 511
- twist_state: float32 [512, 3], P(('ax', 'az')), may hold values from -4 to 4
- leaving_slot: int32 [32768], P(('ax', 'az')), may hold values from 0 to 8191, as said below
- leaving_dest: int32 [32768, 1], P(('ax', 'az')), may hold values from 0 to 127; in each aligned block of 256 rows (0 to 255, 256 to 511, ...) at most 4 rows name the same one
- arrival_slot: int32 [65536], P(('ax', 'az')), may hold values from 0 to 8191, as said below
Outputs:
- particles_out: float32 [32, 256, 128, 128], P('ax', 'az')
- density: float32 [32, 256, 128], P('ax', 'az')
The draws below stay inside these ranges and needn't reach their ends.
Inputs may be any that keep to these rules, and one draw needn't show every extreme that they name: `particles`: rows 0 to 2 lie in [0, 1), row 6 in [0.02, 0.06], row 7 in [0.2, 2]. `pair_codes`: each cell's list holds 6 different codes; the first is 4, the cell itself. `leaving_slot`: the 256 slots of one device are different. `leaving_dest`: devices in mesh order, ax slowest; at most 4 of one device's 256 rows name the same device. `arrival_slot`: the 512 entries of one receiving device are different slots.
All inputs are finite; a program needn't handle non-finite values.
Results may differ from the reference program's by a relative error of at most 0.0003.
Values sent between devices are 32-bit elements; how exact they have to be, the bound alone decides.
No kernel may reach another device: no remote copies, remote signals or barrier semaphores. Data moves between devices by JAX's collectives and lax.ppermute only.
A program may use at most 192 MiB of HBM per device.

```python
import math
import jax
import jax.numpy as jnp
import numpy as np
from jax import lax

CELLS_A = 4
CELLS_Z = 16
SPECIES = 120
BLOCK = 128
PARTNERS = 6
CAP = 4
RANKS = 128
NA = 32
NZ = 256
LEAVING = 256
SEGMENTS = 512
N_AX = 8
N_AZ = 16


def draw_particles(key, part):
    key_list = jax.random.split(key, 6)
    position = jax.random.uniform(key_list[0], (NA, NZ, 3, BLOCK), jnp.float32, 0.0, 0.999)
    motion = 0.5 * jax.random.normal(key_list[1], (NA, NZ, 3, BLOCK), jnp.float32)
    species = jax.random.normal(key_list[3], (NA, NZ, SPECIES, BLOCK), jnp.float32)
    motion = jnp.clip(motion, -3.0, 3.0)
    species = jnp.clip(species, -8.0, 8.0)
    masses = jnp.exp(jax.random.uniform(key_list[2], (NA, NZ, 1, BLOCK), jnp.float32, math.log(0.02), math.log(0.06)))
    viscous = jnp.exp(jax.random.uniform(key_list[5], (NA, NZ, 1, BLOCK), jnp.float32, math.log(0.2), math.log(2.0)))
    return jnp.concatenate([position, motion, masses, viscous, species], axis=2)


def draw_pair_codes(key, part):
    scores = jax.random.randint(key, (NA, NZ, 8), 0, 1048576) * 8 + jnp.arange(8, dtype=jnp.int32)
    ranking = jnp.argsort(scores, axis=-1)[:, :, :PARTNERS - 1].astype(jnp.int32)
    others = ranking + (ranking >= 4).astype(jnp.int32)
    itself = jnp.full((NA, NZ, 1), 4, jnp.int32)
    return jnp.concatenate([itself, others], axis=2)


def draw_leaving_slot(key, part):
    slots_device = CELLS_A * CELLS_Z * BLOCK
    sub_keys = jax.random.split(jax.random.fold_in(key, 11), N_AX * N_AZ)
    chosen = jax.vmap(lambda sub_key: jax.random.permutation(sub_key, slots_device)[:LEAVING])(sub_keys)
    return chosen.reshape(-1).astype(jnp.int32)


def draw_arrival_slot(key, part):
    slots_device = CELLS_A * CELLS_Z * BLOCK
    sub_keys = jax.random.split(jax.random.fold_in(key, 23), N_AX * N_AZ)
    chosen = jax.vmap(lambda sub_key: jax.random.permutation(sub_key, slots_device)[:N_AX * N_AZ * CAP])(sub_keys)
    return chosen.reshape(-1).astype(jnp.int32)


def plant(values, stream_key, low, top_value):
    place = [jax.random.randint(jax.random.fold_in(stream_key, axis), (), 0, length) for axis, length in enumerate(values.shape)]
    widest = values.shape.index(max(values.shape))
    next_to = place[:widest] + [(place[widest] + 1) % values.shape[widest]] + place[widest + 1:]
    return values.at[tuple(place)].set(low).at[tuple(next_to)].set(top_value)


def levels(own_key, dims, cuts, least, largest):
    factor_of = 1.0
    for dim, shards_of in cuts:
        steps = jax.random.uniform(jax.random.fold_in(jax.random.fold_in(own_key, 6), dim), (shards_of,), jnp.float32, least / len(cuts), largest / len(cuts))
        factor_of = factor_of * jnp.repeat(jnp.exp(steps), dims[dim] // shards_of).reshape((-1,) + (1,) * (len(dims) - 1 - dim))
    return factor_of


def deal_out(key, own, number, rows, count, top, bound, skew):
    sequence = jax.random.permutation(key, count)
    heavy_load, common = load_shares(count, rows * top, bound, skew, True), load_shares(count, rows * top, bound, skew, False)
    places = jnp.arange(count)

    def named(tallies, offset_by):
        used = int((tallies > 0).sum())
        fixed = max(1, used // 4)
        passed = fixed + (places - fixed + offset_by * (used - fixed)) % max(1, count - fixed)
        return jnp.zeros((count,), jnp.int32).at[sequence[jnp.where(places < fixed, places, passed)]].set(jnp.asarray(tallies, jnp.int32))

    tallies = jnp.where(number % 4 == 0, named(heavy_load, number // 4), named(common, number - number // 4 - 1))
    mixed = jax.random.permutation(jax.random.fold_in(own, 3), count)
    donor, taker = mixed[0:count // 2 * 2:2], mixed[1:count // 2 * 2:2]
    slack = jnp.minimum(tallies[donor] - 1, bound - tallies[taker]) // 2
    slack = jnp.where((donor == sequence[0]) | (taker == sequence[0]) | (tallies[taker] == 0), 0, jnp.maximum(slack, 0))
    passed = jax.random.randint(jax.random.fold_in(own, 4), (count // 2,), 0, 1 << 20) % (slack + 1)
    tallies = tallies.at[donor].add(-passed).at[taker].add(passed)
    items = jnp.searchsorted(jnp.cumsum(tallies), jnp.arange(rows * top), side="right").astype(jnp.int32)
    listing = items.reshape(top, rows).T
    listing = listing[jax.random.permutation(jax.random.fold_in(own, 1), rows)]
    offset_by = jax.random.randint(jax.random.fold_in(own, 2), (rows, 1), 0, top)
    return jnp.take_along_axis(listing, (jnp.arange(top)[None, :] + offset_by) % top, axis=1)


def load_shares(amount, total, reach, lean, full):
    portions = [(1 << 20) // math.isqrt(standing ** lean) + 1 for standing in range(1, amount + 1)]
    largest = reach if full else min(reach, max(-(-total // amount), total * portions[0] // sum(portions)))
    least = 1 if total - largest >= amount - 1 else 0
    given, surplus = [largest] + [least] * (amount - 1), total - largest - least * (amount - 1)
    while surplus > 0:
        candidates = [i for i in range(1, amount) if given[i] < largest] or [i for i in range(1, amount) if given[i] < reach]
        pool, remaining = sum([portions[i] for i in candidates]), surplus
        for i in candidates:
            addition = min(reach - given[i], max(1, remaining * portions[i] // pool), surplus)
            given[i] = given[i] + addition
            surplus = surplus - addition
    return np.array(given)


def gaussian(stream_key, dims, scale, most, shards=(), held_as=jnp.bfloat16):
    result = jax.random.normal(stream_key, dims, jnp.float32) * scale
    if len(shards) > 0:
        result = levels(stream_key, dims, shards, -0.22, 0.18) * result
    return jnp.clip(result, min=-most, max=most).astype(held_as)


def setup_inputs(seed: int = 0) -> dict:
    key_of = jax.random.split(jax.random.key(seed), 9)
    particles = draw_particles(jax.random.fold_in(key_of[8], 71), 0)
    counts = plant(jax.random.randint(key_of[1], (NA, NZ), 48, 129), jax.random.fold_in(key_of[1], 1), 48, 128).astype(jnp.int32)
    pair_codes = draw_pair_codes(jax.random.fold_in(key_of[8], 71), 0)
    contact = plant(jax.random.randint(key_of[3], (NA, NZ), 0, SEGMENTS), jax.random.fold_in(key_of[3], 1), 0, SEGMENTS - 1).astype(jnp.int32)
    twist_state = gaussian(key_of[4], (SEGMENTS, 3), 1.0, 4.0, ((0, 128),), jnp.float32)
    leaving_slot = draw_leaving_slot(jax.random.fold_in(key_of[8], 71), 0)
    leaving_dest_keys = jax.random.split(jax.random.fold_in(key_of[6], 1), (RANKS * LEAVING) // LEAVING)
    leaving_dest_turns = jax.random.permutation(jax.random.fold_in(key_of[6], 3), (RANKS * LEAVING) // LEAVING)
    leaving_dest = jax.vmap(lambda own, number: deal_out(jax.random.fold_in(key_of[6], 2), own, number, LEAVING, RANKS, 1, CAP, 2))(leaving_dest_keys, leaving_dest_turns).reshape((RANKS * LEAVING, 1))
    arrival_slot = draw_arrival_slot(jax.random.fold_in(key_of[8], 71), 0)
    return dict(particles=particles, counts=counts, pair_codes=pair_codes, contact=contact, twist_state=twist_state, leaving_slot=leaving_slot, leaving_dest=leaving_dest, arrival_slot=arrival_slot)


sound_square = 1.0
wall_gain = 4.0
mix_gain = 2.0
time_step = 0.05


def shifts(code_list):
    return (code_list // 3 - 1).astype(jnp.float32), (code_list % 3 - 1).astype(jnp.float32)


def neighbor_index(code_list, margin, row_width):
    first_row = lax.broadcasted_iota(jnp.int32, code_list.shape, 0)
    second_col = lax.broadcasted_iota(jnp.int32, code_list.shape, 1)
    return (first_row + margin + code_list // 3 - 1) * row_width + second_col + margin + code_list % 3 - 1


def geometry(center, partner, shift_a, shift_z):
    diff_a = partner[..., 0, None, :] + shift_a[..., None, None] - center[..., 0, :, None]
    diff_z = partner[..., 1, None, :] + shift_z[..., None, None] - center[..., 1, :, None]
    diff_y = partner[..., 2, None, :] - center[..., 2, :, None]
    nearness = jnp.maximum(1.0 - (diff_a * diff_a + diff_z * diff_z + diff_y * diff_y), 0.0)
    return (diff_a, diff_z, diff_y), nearness


def density_term(nearness, partner):
    return jnp.sum(nearness * nearness * nearness * partner[..., 6, None, :], axis=-1)


def pressure_terms(density, mass):
    living = mass > 0.0
    guarded = jnp.where(living, density, 1.0)
    press_ratio = jnp.where(living, sound_square * (density - 1.0) / (guarded * guarded), 0.0)
    inverse = jnp.where(living, 1.0 / guarded, 0.0)
    return press_ratio, inverse


def force_terms(center, partner, offsets, nearness, press_center, press_partner, inverse_partner):
    partner_mass = partner[..., 6, None, :]
    square = nearness * nearness
    repulse = partner_mass * (press_center[..., :, None] + press_partner[..., None, :]) * 6.0 * square
    friction = partner_mass * inverse_partner[..., None, :] * (center[..., 7, :, None] + partner[..., 7, None, :]) * square
    acceleration = -jnp.stack([jnp.sum(repulse * component, axis=-1) for component in offsets], axis=-2)
    acceleration = acceleration + jnp.einsum("...ij,...cj->...ci", friction, partner[..., 3:6, :], precision=lax.Precision.HIGHEST) - center[..., 3:6, :] * jnp.sum(friction, axis=-1)[..., None, :]
    mixing = mix_gain * partner_mass * inverse_partner[..., None, :] * square
    mixing_rate = jnp.einsum("...ij,...cj->...ci", mixing, partner[..., 8:, :], precision=lax.Precision.HIGHEST) - center[..., 8:, :] * jnp.sum(mixing, axis=-1)[..., None, :]
    return acceleration, mixing_rate


def advance(center, acceleration, mixing_rate, surface):
    living = (center[..., 6, :] > 0.0).astype(jnp.float32)[..., None, :]
    wall_weight = jnp.maximum(1.0 - 3.0 * center[..., 2, :], 0.0)[..., None, :]
    wall_pull = wall_gain * wall_weight * (surface[..., :, None] - center[..., 3:6, :])
    velocity = center[..., 3:6, :] + time_step * (acceleration + wall_pull) * living
    position = center[..., 0:3, :] + time_step * velocity
    species = center[..., 8:, :] + time_step * mixing_rate * living
    return jnp.concatenate([position, velocity, center[..., 6:8, :], species], axis=-2)


def wrap_pad(field):
    extended = jnp.concatenate([field[:, -1:], field, field[:, :1]], axis=1)
    zero_rows = jnp.zeros_like(extended[:1])
    return jnp.concatenate([zero_rows, extended, zero_rows], axis=0)


def global_step(current, pair_codes, surface):
    grid_rows, grid_cols, fields, block_size = current.shape
    flat_cells = wrap_pad(current).reshape(-1, fields, block_size)
    partner_index = neighbor_index(pair_codes, 1, grid_cols + 2)
    shift_a, shift_z = shifts(pair_codes)
    members = pair_codes.shape[2]

    def row_density(row_number):
        center = current[row_number]
        running = jnp.zeros((grid_cols, block_size), jnp.float32)
        for member in range(members):
            partner = flat_cells[partner_index[row_number, :, member]]
            nearness = geometry(center, partner, shift_a[row_number, :, member], shift_z[row_number, :, member])[1]
            running = running + density_term(nearness, partner)
        return running

    density = lax.map(row_density, jnp.arange(grid_rows, dtype=jnp.int32))
    press_ratio, inverse = pressure_terms(density, current[:, :, 6, :])
    flat_pressure = wrap_pad(jnp.stack([press_ratio, inverse], axis=2)).reshape(-1, 2, block_size)

    def row_force(row_number):
        center = current[row_number]
        acceleration = jnp.zeros((grid_cols, 3, block_size), jnp.float32)
        mixing_rate = jnp.zeros((grid_cols, fields - 8, block_size), jnp.float32)
        for member in range(members):
            partner = flat_cells[partner_index[row_number, :, member]]
            partner_press = flat_pressure[partner_index[row_number, :, member]]
            offsets, nearness = geometry(center, partner, shift_a[row_number, :, member], shift_z[row_number, :, member])
            accel_part, mixing_part = force_terms(center, partner, offsets, nearness, press_ratio[row_number], partner_press[:, 0, :], partner_press[:, 1, :])
            acceleration = acceleration + accel_part
            mixing_rate = mixing_rate + mixing_part
        return advance(center, acceleration, mixing_rate, surface[row_number])

    advanced = lax.map(row_force, jnp.arange(grid_rows, dtype=jnp.int32))
    living = (current[:, :, 6, :] > 0.0).astype(jnp.float32)
    return advanced, density * living


def global_migrate(current, leaving_slot, leaving_dest, arrival_slot):
    grid_rows, grid_cols, fields, block_size = current.shape
    ranks_total = N_AX * N_AZ
    local_rows = grid_rows // N_AX
    local_cols = grid_cols // N_AZ
    by_device = current.reshape(N_AX, local_rows, N_AZ, local_cols, fields, block_size)
    by_device = by_device.transpose(0, 2, 1, 3, 4, 5).reshape(ranks_total, local_rows * local_cols, fields, block_size)
    leaving_count = leaving_slot.shape[0] // ranks_total
    source = leaving_slot.reshape(ranks_total, leaving_count)
    dest_rank = leaving_dest[:, 0].reshape(ranks_total, leaving_count)
    onehot = (dest_rank[:, :, None] == jnp.arange(ranks_total, dtype=jnp.int32)[None, None, :]).astype(jnp.int32)
    before = jnp.cumsum(onehot, axis=1) - onehot
    dest_order = jnp.sum(before * onehot, axis=2)
    capacity = arrival_slot.shape[0] // (ranks_total * ranks_total)
    arrival_table = arrival_slot.reshape(ranks_total, ranks_total, capacity)
    sender = jnp.broadcast_to(jnp.arange(ranks_total, dtype=jnp.int32)[:, None], (ranks_total, leaving_count))
    target = arrival_table[dest_rank, sender, dest_order]
    moving = by_device[sender, source // block_size, :, source % block_size]
    by_device = by_device.at[sender, source // block_size, :, source % block_size].set(0.0)
    by_device = by_device.at[dest_rank, target // block_size, :, target % block_size].set(moving)
    by_device = by_device.reshape(N_AX, N_AZ, local_rows, local_cols, fields, block_size).transpose(0, 2, 1, 3, 4, 5)
    return by_device.reshape(grid_rows, grid_cols, fields, block_size)


def reference(particles, counts, pair_codes, contact, twist_state, leaving_slot, leaving_dest, arrival_slot):
    slot_iota = lax.broadcasted_iota(jnp.int32, (particles.shape[0], particles.shape[1], particles.shape[3]), 2)
    keep_mask = (slot_iota < counts[:, :, None]).astype(jnp.float32)
    current = particles * keep_mask[:, :, None, :]
    surface = twist_state[contact]
    current, density = global_step(current, pair_codes, surface)
    current = global_migrate(current, leaving_slot, leaving_dest, arrival_slot)
    current, density = global_step(current, pair_codes, surface)
    return current, density
```

```python
import functools

import jax
import jax.numpy as jnp
from jax import lax
from jax.experimental import pallas as pl
from jax.experimental.pallas import tpu as pltpu
from jax.sharding import PartitionSpec as P

AXES = ("ax", "az")
F32, BF16, I32 = jnp.float32, jnp.bfloat16, jnp.int32

wall_gain = 4.0
time_step = 0.05
MIB = 1 << 20


def rows_of(x, n):
    return jnp.broadcast_to(x, (n,) + x.shape[1:])


def sub_iota(shape):
    return lax.broadcasted_iota(I32, shape, 0)


def halves(x):
    hi = x.astype(BF16)
    return hi, (x - hi.astype(F32)).astype(BF16)


def thirds(x):
    hi = x.astype(BF16).astype(F32)
    rest = x - hi
    mid = rest.astype(BF16).astype(F32)
    return hi, mid, rest - mid


def step_kernel(rows, cols, tab, surf, *refs):
    (cells, a_low, a_high, z_low, z_high, c_ll, c_lh, c_hl, c_hh, out, dens, side_t, side_s, feat, squares, mass, root, rho, ratio, inverse) = refs
    width = cols + 4
    sub8 = sub_iota((8, 128))
    eye = (sub_iota((128, 128)) == lax.broadcasted_iota(I32, (128, 128), 1)).astype(F32).astype(BF16)
    zero_b = jnp.zeros((64, 128), BF16)
    row_mid, col_mid = (rows + 3) / 2.0, (cols + 3) / 2.0

    def shifted(g, r, c):
        off_r = r.astype(F32) - row_mid
        off_c = c.astype(F32) - col_mid
        return jnp.where(sub8 == 0, g + off_r, jnp.where(sub8 == 1, g + off_c, g))

    def geometry(g, r, c, center):
        x = jnp.where(sub8 < 3, shifted(g, r, c), 0.0)
        norm = rows_of(jnp.sum(x * x, axis=0, keepdims=True), 8)
        m = rows_of(g[6:7], 8)
        cube = jnp.exp2(jnp.log2(jnp.maximum(m, 1e-30)) * (1.0 / 3.0))
        cube = cube - (cube - m / (cube * cube)) * (1.0 / 3.0)
        cube = jnp.where(m > 0.0, cube, 0.0)
        u = jnp.where(sub8 < 3, x, jnp.where(sub8 == 3, -norm, jnp.where(sub8 == 4, 1.0, 0.0))) * cube
        uh, um, ul = thirds(u)
        zero = jnp.zeros_like(u)
        t_rows = jnp.concatenate([uh, um, ul, uh, um, uh, zero, zero], axis=0).astype(BF16)
        index = r * width + c
        mass[pl.ds(index, 1), :] = g[6:7]
        root[pl.ds(index, 1), :] = cube[0:1]
        if center:
            w = jnp.where(sub8 < 3, x + x, jnp.where(sub8 == 3, 1.0, jnp.where(sub8 == 4, 1.0 - norm, 0.0)))
            wh, wm, wl = thirds(w)
            side_s[index] = jnp.concatenate([wh, wh, wh, wm, wm, wl, zero, zero], axis=0).astype(BF16)
        return t_rows

    def turned(items):
        for k in range(0, len(items), 2):
            pair = items[k : k + 2]
            blocks = []
            for g, r, c, center in pair:
                blocks += [geometry(g, r, c, center), zero_b]
            if len(pair) == 1:
                blocks += [zero_b, zero_b]
            t = lax.dot_general(eye, jnp.concatenate(blocks, axis=0), (((1,), (1,)), ((), ())), preferred_element_type=F32)
            for n, (g, r, c, center) in enumerate(pair):
                side_t[r * width + c] = t[:, n * 128 : (n + 1) * 128].astype(BF16)

    def loop(n, body):
        def step(i, carry):
            body(i)
            return carry

        lax.fori_loop(0, n, step, 0)

    unroll = 4

    def local_geo(i):
        items = []
        for k in range(unroll):
            n = i * unroll + k
            items.append((cells[n, 0:8, :], n // cols + 2, n % cols + 2, True))
        turned(items)

    loop(rows * cols // unroll, local_geo)

    def a_geo(ref, first, second, i):
        items = []
        for k in range(2):
            n = i * 2 + k
            items.append((ref[n, 0:8, :], jnp.int32(first), n + 2, True))
            items.append((ref[n, 128:136, :], jnp.int32(second), n + 2, False))
        turned(items)

    loop(cols // 2, functools.partial(a_geo, a_low, 1, 0))
    loop(cols // 2, functools.partial(a_geo, a_high, rows + 2, rows + 3))

    def z_geo(ref, first, second, i):
        turned([(ref[i, 0:8, :], i + 2, jnp.int32(first), True), (ref[i, 128:136, :], i + 2, jnp.int32(second), False)])

    loop(rows, functools.partial(z_geo, z_low, 1, 0))
    loop(rows, functools.partial(z_geo, z_high, cols + 2, cols + 3))
    corners = ((c_ll, 1, 0, 1, 0), (c_lh, 1, 0, cols + 2, cols + 3), (c_hl, rows + 2, rows + 3, 1, 0), (c_hh, rows + 2, rows + 3, cols + 2, cols + 3))
    for ref, r1, r0, k1, k0 in corners:
        r1, r0, k1, k0 = jnp.int32(r1), jnp.int32(r0), jnp.int32(k1), jnp.int32(k0)
        turned([(ref[0, 0:8, :], r1, k1, True), (ref[0, 128:136, :], r0, k1, False), (ref[0, 136:144, :], r1, k0, False), (ref[0, 144:152, :], r0, k0, False)])

    zero_w = jnp.zeros((64, 128), BF16)
    zero_h = jnp.zeros((128, 128), BF16)

    def density(n, keep):
        base = n * 8
        center = tab[base]
        b = jnp.concatenate([side_s[center], zero_w], axis=0)
        rhs = jnp.concatenate([jnp.concatenate([b, zero_h], axis=1), jnp.concatenate([zero_h, b], axis=1)], axis=0)
        total = jnp.zeros((8, 128), F32)
        for j in range(3):
            lhs = jnp.concatenate([side_t[tab[base + 1 + 2 * j]], side_t[tab[base + 2 + 2 * j]]], axis=1)
            y = jnp.maximum(jnp.dot(lhs, rhs, preferred_element_type=F32), 0.0)
            square = y * y
            cubes = square * y
            for h in range(2):
                lanes = slice(h * 128, (h + 1) * 128)
                total = total + jnp.sum(cubes[:, lanes].reshape(16, 8, 128), axis=0)
                if keep:
                    squares[n, j * 256 + h * 128 : j * 256 + (h + 1) * 128, :] = square[:, lanes].astype(BF16)
        rho[pl.ds(center, 1), :] = jnp.sum(total, axis=0, keepdims=True)

    own = rows * cols
    ring = 2 * (rows + 2) + 2 * cols

    def own_density(i):
        for k in range(2):
            density(i * 2 + k, True)

    loop(own // 2, own_density)

    def ring_density(i):
        for k in range(2):
            density(own + i * 2 + k, False)

    loop(ring // 2, ring_density)

    living = mass[...] > 0.0
    guarded = jnp.where(living, rho[...], 1.0)
    ratio[...] = jnp.where(living, (guarded - 1.0) / (guarded * guarded), 0.0)
    inverse[...] = jnp.where(living, 1.0 / guarded, 0.0)

    def row8(ref, index):
        return rows_of(ref[pl.ds(index, 1), :], 8)

    def positions(g, r, c):
        x = shifted(g, r, c)
        return jnp.where((sub8 == 0) | (sub8 == 4), 1.0, jnp.where(sub8 < 4, pltpu.roll(x, 1, 0), pltpu.roll(x, 5, 0)))

    def features(load, r, c):
        index = r * width + c
        g = load(0)
        cube = row8(root, index)
        scale = cube * row8(inverse, index)
        nu = rows_of(g[7:8], 8)
        first = jnp.where(sub8 < 3, pltpu.roll(g, 5, 0) * nu, jnp.where(sub8 == 6, 1.0, g)) * scale
        press = positions(g, r, c) * jnp.where(sub8 < 4, cube, cube * row8(ratio, index))
        hi, lo = halves(press)
        feat[index, 128:144, :] = jnp.concatenate([hi.astype(F32), lo.astype(F32)], axis=0).astype(BF16)
        feat[index, 0:16, :] = jnp.concatenate([first, load(1) * scale], axis=0).astype(BF16)
        for k in range(1, 8):
            feat[index, 16 * k : 16 * k + 16, :] = jnp.concatenate([load(2 * k) * scale, load(2 * k + 1) * scale], axis=0).astype(BF16)

    def loader(ref, n):
        return lambda k: ref[n, 8 * k : 8 * k + 8, :]

    def local_feat(i):
        for k in range(2):
            n = i * 2 + k
            features(loader(cells, n), n // cols + 2, n % cols + 2)

    loop(own // 2, local_feat)

    def a_feat(i):
        features(loader(a_low, i), jnp.int32(1), i + 2)
        features(loader(a_high, i), jnp.int32(rows + 2), i + 2)

    loop(cols, a_feat)

    def z_feat(i):
        features(loader(z_low, i), i + 2, jnp.int32(1))
        features(loader(z_high, i), i + 2, jnp.int32(cols + 2))

    loop(rows, z_feat)
    for ref, r1, r0, k1, k0 in corners:
        features(loader(ref, 0), jnp.int32(r1), jnp.int32(k1))

    def force(n):
        r, c = n // cols + 2, n % cols + 2
        index = r * width + c
        base = n * 8
        lhs = jnp.concatenate([feat[tab[base + 1 + j]] for j in range(6)], axis=1)
        sums = jnp.dot(lhs, squares[n], preferred_element_type=F32)
        g = cells[n, 0:8, :]
        m, nu = rows_of(g[6:7], 8), rows_of(g[7:8], 8)
        alive = jnp.where(m > 0.0, time_step, 0.0)
        first = sums[0:8]
        press = sums[128:136] + sums[136:144]
        press = press - positions(g, r, c) * jnp.where(sub8 < 4, rows_of(press[0:1], 8), rows_of(press[4:5], 8))
        press = press * jnp.where(sub8 < 4, row8(ratio, index), 1.0)
        press = press + pltpu.roll(press, 4, 0)
        weight, friction = rows_of(first[6:7], 8), rows_of(first[7:8], 8)
        surface = jnp.where(sub8 == 3, surf[n * 4], jnp.where(sub8 == 4, surf[n * 4 + 1], surf[n * 4 + 2]))
        wall = wall_gain * jnp.maximum(1.0 - 3.0 * rows_of(g[2:3], 8), 0.0)
        accel = nu * (first - g * weight) + pltpu.roll(first, 3, 0) - g * friction + wall * (surface - g)
        accel = accel - 6.0 * pltpu.roll(press, 2, 0)
        velocity = g + accel * alive
        position = g + time_step * pltpu.roll(velocity, 5, 0)
        out[n, 0:8, :] = jnp.where(sub8 < 3, position, jnp.where(sub8 < 6, velocity, g))
        gain = 2.0 * alive
        stay = 1.0 - gain * weight
        for k in range(1, 16):
            out[n, 8 * k : 8 * k + 8, :] = cells[n, 8 * k : 8 * k + 8, :] * stay + gain * sums[8 * k : 8 * k + 8]
        dens[pl.ds(n, 1), :] = jnp.where(m > 0.0, row8(rho, index), 0.0)[0:1]

    def forces(i):
        for k in range(2):
            force(i * 2 + k)

    loop(own // 2, forces)


def step_call(rows, cols, table, surface, cells, halo):
    own = rows * cols
    patch = (rows + 4) * (cols + 4)
    smem = pl.BlockSpec(memory_space=pltpu.SMEM)
    vmem = pl.BlockSpec(memory_space=pltpu.VMEM)
    return pl.pallas_call(
        functools.partial(step_kernel, rows, cols),
        out_shape=(jax.ShapeDtypeStruct((own, 128, 128), F32), jax.ShapeDtypeStruct((own, 128), F32)),
        in_specs=[smem, smem] + [vmem] * 9,
        out_specs=(vmem, vmem),
        scratch_shapes=[
            pltpu.VMEM((patch, 128, 128), BF16),
            pltpu.VMEM((patch, 64, 128), BF16),
            pltpu.VMEM((patch, 144, 128), BF16),
            pltpu.VMEM((own, 768, 128), BF16),
            pltpu.VMEM((patch, 128), F32),
            pltpu.VMEM((patch, 128), F32),
            pltpu.VMEM((patch, 128), F32),
            pltpu.VMEM((patch, 128), F32),
            pltpu.VMEM((patch, 128), F32),
        ],
        compiler_params=pltpu.CompilerParams(vmem_limit_bytes=60 * MIB),
    )(table, surface, cells, *halo)


def extract_kernel(state, slots, buffer_row, out, kept, moved):
    cells, leaving, slots_out = state.shape[0], slots.shape[0], out.shape[0]
    offset = jnp.broadcast_to(slots[...], (leaving, 128)) - lax.broadcasted_iota(I32, (leaving, 128), 1)
    moved[...] = jnp.zeros_like(moved)

    def body(c, carry):
        hit = jnp.where(offset == c * 128, 1.0, 0.0)
        gone = jnp.sum(hit, axis=0, keepdims=True)
        hi, lo = halves(state[c])
        moved[...] += lax.dot_general(hit.astype(BF16), jnp.concatenate([hi, lo], axis=0), (((1,), (1,)), ((), ())), preferred_element_type=F32)
        kept[c] = state[c] * (1.0 - gone)
        return carry

    lax.fori_loop(0, cells, body, 0)
    place = jnp.where(jnp.broadcast_to(buffer_row[...], (slots_out, leaving)) == sub_iota((slots_out, leaving)), 1.0, 0.0).astype(BF16)
    right = jnp.concatenate([moved[...].astype(BF16), jnp.ones((leaving, 128), BF16)], axis=1)
    sums = jnp.dot(place, right, preferred_element_type=F32)
    lane = lax.broadcasted_iota(I32, (slots_out, 128), 1)
    out[...] = jnp.where((lane == 6) & (sums[:, 256:384] < 0.5), -1.0, sums[:, 0:128] + sums[:, 128:256])


def extract(state, slots, buffer_row, places):
    vmem = pl.BlockSpec(memory_space=pltpu.VMEM)
    return pl.pallas_call(
        extract_kernel,
        out_shape=(jax.ShapeDtypeStruct((places, 128), F32), jax.ShapeDtypeStruct(state.shape, F32)),
        in_specs=[vmem] * 3,
        out_specs=(vmem, vmem),
        scratch_shapes=[pltpu.VMEM((slots.shape[0], 256), F32)],
        compiler_params=pltpu.CompilerParams(vmem_limit_bytes=40 * MIB),
    )(state, slots, buffer_row)


def insert_kernel(state, incoming, slots, out):
    cells, places = state.shape[0], slots.shape[0]
    data = incoming[...]
    absent = jnp.broadcast_to(data[:, 6:7], (places, 128)) < 0.0
    offset = jnp.broadcast_to(slots[...], (places, 128)) - lax.broadcasted_iota(I32, (places, 128), 1)
    offset = jnp.where(absent, -1, offset)
    hi, lo = halves(jnp.transpose(data))
    left = jnp.concatenate([hi, lo, jnp.ones((16, places), BF16)], axis=0)

    def body(i, carry):
        hits = [jnp.where(offset == (2 * i + k) * 128, 1.0, 0.0).astype(BF16) for k in range(2)]
        sums = jnp.dot(left, jnp.concatenate(hits, axis=1), preferred_element_type=F32)
        for k in range(2):
            part = sums[:, 128 * k : 128 * (k + 1)]
            out[2 * i + k] = state[2 * i + k] * (1.0 - part[256:257]) + (part[0:128] + part[128:256])
        return carry

    lax.fori_loop(0, cells // 2, body, 0)


def insert(state, incoming, slots):
    vmem = pl.BlockSpec(memory_space=pltpu.VMEM)
    return pl.pallas_call(
        insert_kernel,
        out_shape=jax.ShapeDtypeStruct(state.shape, F32),
        in_specs=[vmem] * 3,
        out_specs=vmem,
        compiler_params=pltpu.CompilerParams(vmem_limit_bytes=40 * MIB),
    )(state, incoming, slots)


def moves(n_ax, n_az, da, dz):
    pairs = []
    for a in range(n_ax):
        for z in range(n_az):
            if 0 <= a + da < n_ax:
                pairs.append((a * n_az + z, (a + da) * n_az + (z + dz) % n_az))
    return pairs


def rim(state, rows, cols, n_ax, n_az):
    grid = state.reshape(rows, cols, 128, 128)

    def ax_part(first, second):
        return jnp.concatenate([grid[first], grid[second, :, 0:8]], axis=1)

    def az_part(first, second):
        return jnp.concatenate([grid[:, first], grid[:, second, 0:8]], axis=1)

    def corner(r1, r0, k1, k0):
        return jnp.concatenate([grid[r1, k1], grid[r0, k1, 0:8], grid[r1, k0, 0:8], grid[r0, k0, 0:8]], axis=0)[None]

    lo, hi = (0, 1), (-1, -2)
    sent = [
        (ax_part(*hi), 1, 0),
        (ax_part(*lo), -1, 0),
        (az_part(*hi), 0, 1),
        (az_part(*lo), 0, -1),
        (corner(*hi, *hi), 1, 1),
        (corner(*hi, *lo), 1, -1),
        (corner(*lo, *hi), -1, 1),
        (corner(*lo, *lo), -1, -1),
    ]
    return [lax.ppermute(x, AXES, moves(n_ax, n_az, da, dz)) for x, da, dz in sent]


def border(rows, cols):
    cells = [(r, c) for r in range(rows) for c in range(cols) if r in (0, rows - 1) or c in (0, cols - 1)]
    return cells, {cell: n for n, cell in enumerate(cells)}


def local(particles, counts, pair_codes, contact, twist_state, leaving_slot, leaving_dest, arrival_slot):
    rows, cols, fields, block = particles.shape
    n_ax, n_az = lax.axis_size("ax"), lax.axis_size("az")
    ranks = n_ax * n_az
    own = rows * cols
    ax, az = lax.axis_index("ax"), lax.axis_index("az")

    keep = lax.broadcasted_iota(I32, (own, block), 1) < counts.reshape(own, 1)
    state = jnp.where(keep[:, None, :], particles.reshape(own, fields, block), 0.0)
    halo = rim(state, rows, cols, n_ax, n_az)

    listed, place = border(rows, cols)
    partners = pair_codes.shape[2]
    rim_codes = jnp.stack([pair_codes[r, c] for r, c in listed]).astype(F32)
    segments = twist_state.shape[0]
    used = segments * 3 + len(listed) * partners
    padded = -(-used // 128) * 128
    packed = jnp.concatenate([twist_state.reshape(-1), rim_codes.reshape(-1), jnp.zeros((padded - used,), F32)])
    everyone = lax.all_gather(packed.reshape(-1, 128), AXES).reshape(ranks, padded)
    twist = everyone[:, : segments * 3].reshape(ranks * segments, 3)
    surface = jnp.pad(twist[contact.reshape(own)], ((0, 0), (0, 1))).reshape(-1)
    codes = everyone[:, segments * 3 : used].reshape(ranks * len(listed), partners)

    ring = [(r, c) for r in range(-1, rows + 1) for c in range(-1, cols + 1) if not (0 <= r < rows and 0 <= c < cols)]
    side_a = jnp.array([-1 if r < 0 else (1 if r >= rows else 0) for r, c in ring], I32)
    side_z = jnp.array([-1 if c < 0 else (1 if c >= cols else 0) for r, c in ring], I32)
    number = jnp.array([place[(r % rows, c % cols)] for r, c in ring], I32)
    device = jnp.clip(ax + side_a, 0, n_ax - 1) * n_az + (az + side_z) % n_az
    ring_codes = codes[device * len(listed) + number].astype(I32)

    width = cols + 4
    centers = jnp.array([(r + 2) * width + c + 2 for r in range(rows) for c in range(cols)] + [(r + 2) * width + c + 2 for r, c in ring], I32)
    all_codes = jnp.concatenate([pair_codes.reshape(own, partners), ring_codes], axis=0)
    linked = centers[:, None] + (all_codes // 3 - 1) * width + all_codes % 3 - 1
    table = jnp.concatenate([centers[:, None], linked, jnp.zeros((centers.shape[0], 1), I32)], axis=1).reshape(-1)

    dest = leaving_dest[:, 0]
    leaving = dest.shape[0]
    same = dest[:, None] == dest[None, :]
    earlier = lax.broadcasted_iota(I32, (leaving, leaving), 0) > lax.broadcasted_iota(I32, (leaving, leaving), 1)
    order = jnp.sum((same & earlier).astype(I32), axis=1)
    capacity = arrival_slot.shape[0] // ranks
    buffer_row = (dest * capacity + order).reshape(1, leaving)

    state, _ = step_call(rows, cols, table, surface, state, halo)
    outgoing, state = extract(state, leaving_slot.reshape(-1, 1), buffer_row, ranks * capacity)
    incoming = lax.all_to_all(outgoing.reshape(ranks, capacity, fields), AXES, 0, 0, tiled=True)
    state = insert(state, incoming.reshape(-1, fields), arrival_slot.reshape(-1, 1))
    halo = rim(state, rows, cols, n_ax, n_az)
    state, density = step_call(rows, cols, table, surface, state, halo)
    return state.reshape(particles.shape), density.reshape(rows, cols, block)


def solution(mesh):
    both = P("ax", "az")
    flat = P(AXES)
    return jax.shard_map(
        local,
        mesh=mesh,
        in_specs=(P("ax", "az", None, None), both, P("ax", "az", None), both, P(AXES, None), flat, P(AXES, None), flat),
        out_specs=(P("ax", "az", None, None), P("ax", "az", None)),
        check_vma=False,
    )
```

```python
import functools

import jax
import jax.numpy as jnp
from jax import lax
from jax.experimental import pallas as pl
from jax.experimental.pallas import tpu as pltpu
from jax.sharding import PartitionSpec as P

AXES = ("ax", "az")
F32, BF16, I32 = jnp.float32, jnp.bfloat16, jnp.int32

wall_gain = 4.0
time_step = 0.05
MIB = 1 << 20


def rows_of(x, n):
    return jnp.broadcast_to(x, (n,) + x.shape[1:])


def sub_iota(shape):
    return lax.broadcasted_iota(I32, shape, 0)


def halves(x):
    hi = x.astype(BF16)
    return hi, (x - hi.astype(F32)).astype(BF16)


def thirds(x):
    hi = x.astype(BF16).astype(F32)
    rest = x - hi
    mid = rest.astype(BF16).astype(F32)
    return hi, mid, rest - mid


def loop(n, body):
    def step(i, carry):
        body(i)
        return carry

    lax.fori_loop(0, n, step, 0)


ROWS_K = 32
CODE_ROW = 135


def step_kernel(rows, cols, leaving, codes, surf, *refs):
    (cells, a_low, a_high, z_low, z_high, corner_low, corner_high) = refs[:7]
    if leaving:
        slots, buffer_row, out, sent, gathered = refs[7:12]
        scratch = refs[12:]
    else:
        out, dens = refs[7:9]
        scratch = refs[9:]
    side_t, side_s, feat, squares, row_t, row_s, mass, root, rho, ratio, inverse, ring_codes, semaphore = scratch
    width = cols + 4
    own = rows * cols
    sub8 = sub_iota((8, 128))
    eye = (sub_iota((128, 128)) == lax.broadcasted_iota(I32, (128, 128), 1)).astype(F32).astype(BF16)
    row_mid, col_mid = (rows + 3) / 2.0, (cols + 3) / 2.0

    parts = ((a_low, 0, cols), (a_high, cols, cols), (z_low, 2 * cols, rows), (z_high, 2 * cols + rows, rows), (corner_low, 2 * cols + 2 * rows, 2), (corner_high, 2 * cols + 2 * rows + 2, 2))
    copies = [pltpu.make_async_copy(ref.at[:, CODE_ROW, :], ring_codes.at[pl.ds(first, n), :], semaphore.at[k]) for k, (ref, first, n) in enumerate(parts)]
    for copy in copies:
        copy.start()

    def geometry(ref, cell, height, row, n, index, apart, r, c, center):
        flat = ref.reshape(ref.shape[0] * height, 128)

        def field(k):
            return flat[pl.ds(cell * height + row + k, n, stride=height), :]

        x = [field(0) + (r - row_mid), field(1) + (c - col_mid), field(2)]
        norm = x[0] * x[0] + x[1] * x[1] + x[2] * x[2]
        m = field(6)
        cube = jnp.exp2(jnp.log2(jnp.maximum(m, 1e-30)) * (1.0 / 3.0))
        cube = cube - (cube - m / (cube * cube)) * (1.0 / 3.0)
        cube = jnp.where(m > 0.0, cube, 0.0)

        def put(target, k, value):
            target[pl.ds(index * ROWS_K + k, n, stride=apart * ROWS_K), :] = value

        for k, value in enumerate([x[0] * cube, x[1] * cube, x[2] * cube, -norm * cube, cube]):
            hi, mid, low = thirds(value)
            for block, piece in enumerate((hi, mid, low, hi, mid, hi)):
                put(row_t, 5 * block + k, piece)
        put(row_t, 30, jnp.zeros_like(m))
        put(row_t, 31, jnp.zeros_like(m))
        for k in range(n):
            mass[pl.ds(index + k * apart, 1), :] = m[k : k + 1]
            root[pl.ds(index + k * apart, 1), :] = cube[k : k + 1]
        if center:
            for k, value in enumerate([x[0] + x[0], x[1] + x[1], x[2] + x[2], jnp.ones_like(m), 1.0 - norm]):
                hi, mid, low = thirds(value)
                for block, piece in enumerate((hi, hi, hi, mid, mid, low)):
                    put(row_s, 5 * block + k, piece)
            put(row_s, 30, jnp.zeros_like(m))
            put(row_s, 31, jnp.zeros_like(m))

    def sub(n):
        return sub_iota((n, 128)).astype(F32)

    per = 8

    def local_geo(i):
        first = i * per
        r, c = first // cols + 2, first % cols + 2
        geometry(cells, first, 128, 0, per, r * width + c, 1, r.astype(F32), c.astype(F32) + sub(per), True)

    loop(own // per, local_geo)
    for ref, first, second in ((a_low, 1, 0), (a_high, rows + 2, rows + 3)):
        for k in range(0, cols, per):
            c = k + 2.0 + sub(per)
            geometry(ref, k, 136, 0, per, first * width + k + 2, 1, float(first), c, True)
            geometry(ref, k, 136, 128, per, second * width + k + 2, 1, float(second), c, False)
    for ref, first, second in ((z_low, 1, 0), (z_high, cols + 2, cols + 3)):
        r = 2.0 + sub(rows)
        geometry(ref, 0, 136, 0, rows, 2 * width + first, width, r, float(first), True)
        geometry(ref, 0, 136, 128, rows, 2 * width + second, width, r, float(second), False)
    for ref, k1, k0 in ((corner_low, 1, 0), (corner_high, cols + 2, cols + 3)):
        for n, (r1, r0) in enumerate(((1, 0), (rows + 2, rows + 3))):
            for row, r, k, center in ((0, r1, k1, True), (128, r0, k1, False), (136, r1, k0, False), (144, r0, k0, False)):
                geometry(ref, n, 152, row, 1, r * width + k, 1, float(r), float(k), center)

    def block32(ref, index):
        return ref[pl.ds(pl.multiple_of(index * ROWS_K, ROWS_K), ROWS_K), :].astype(BF16)

    zero_t = jnp.zeros((96, 128), BF16)
    turns = 10

    def turn(i):
        for k in range(turns // 2):
            index = i * turns + 2 * k
            rhs = jnp.concatenate([block32(row_t, index), zero_t, block32(row_t, index + 1), zero_t], axis=0)
            t = lax.dot_general(eye, rhs, (((1,), (1,)), ((), ())), preferred_element_type=F32)
            for n in range(2):
                side_t[index + n] = t[:, n * 128 : (n + 1) * 128].astype(BF16)
                side_s[index + n] = block32(row_s, index + n)

    loop((rows + 4) * width // turns, turn)

    for copy in copies:
        copy.wait()
    zero_s = jnp.zeros((96, 128), BF16)

    def density(center, partners, n):
        rhs = jnp.concatenate([side_s[center], zero_s], axis=0)
        total = jnp.zeros((8, 128), F32)
        for j, partner in enumerate(partners):
            y = jnp.maximum(jnp.dot(side_t[partner], rhs, preferred_element_type=F32), 0.0)
            square = y * y
            total = total + jnp.sum((square * y).reshape(16, 8, 128), axis=0)
            if n is not None:
                squares[n, j * 128 : (j + 1) * 128, :] = square.astype(BF16)
        rho[pl.ds(center, 1), :] = jnp.sum(total, axis=0, keepdims=True)

    def linked(center, code):
        up = (code * 11) >> 5
        return center + up * (width - 3) + code - (width + 1)

    def own_cell(n):
        r, c = n // cols, n % cols
        center = (r + 2) * width + c + 2
        return r, c, center, [linked(center, codes[r, c, j]) for j in range(6)]

    def own_density(i):
        for k in range(8):
            n = i * 8 + k
            r, c, center, partners = own_cell(n)
            density(center, partners, n)

    loop(own // 8, own_density)

    def ring_cell(center, n):
        density(center, [linked(center, ring_codes[n, j].astype(I32)) for j in range(6)], None)

    def a_density(i):
        for k in range(4):
            n = i * 4 + k
            ring_cell(width + n + 2, n)
            ring_cell((rows + 2) * width + n + 2, cols + n)

    loop(cols // 4, a_density)
    for k in range(rows):
        ring_cell((k + 2) * width + 1, 2 * cols + k)
        ring_cell((k + 2) * width + cols + 2, 2 * cols + rows + k)
    for k, r in enumerate((1, rows + 2)):
        ring_cell(r * width + 1, 2 * cols + 2 * rows + k)
        ring_cell(r * width + cols + 2, 2 * cols + 2 * rows + 2 + k)

    living = mass[...] > 0.0
    guarded = jnp.where(living, rho[...], 1.0)
    ratio[...] = jnp.where(living, (guarded - 1.0) / (guarded * guarded), 0.0)
    inverse[...] = jnp.where(living, 1.0 / guarded, 0.0)

    def row8(ref, index):
        return rows_of(ref[pl.ds(index, 1), :], 8)

    def shifted(g, r, c):
        off_r = r.astype(F32) - row_mid
        off_c = c.astype(F32) - col_mid
        return jnp.where(sub8 == 0, g + off_r, jnp.where(sub8 == 1, g + off_c, g))

    def positions(g, r, c):
        x = shifted(g, r, c)
        return jnp.where((sub8 == 0) | (sub8 == 4), 1.0, jnp.where(sub8 < 4, pltpu.roll(x, 1, 0), pltpu.roll(x, 5, 0)))

    def features(ref, n, r, c):
        index = r * width + c
        cube = row8(root, index)
        scale = cube * row8(inverse, index)

        def load(k):
            return ref[n, 8 * k : 8 * k + 8, :]

        g = load(0)
        nu = rows_of(g[7:8], 8)
        first = jnp.where(sub8 < 3, pltpu.roll(g, 5, 0) * nu, jnp.where(sub8 == 6, 1.0, g)) * scale
        press = positions(g, r, c) * jnp.where(sub8 < 4, cube, cube * row8(ratio, index))
        hi, lo = halves(press)
        feat[index, 128:144, :] = jnp.concatenate([hi.astype(F32), lo.astype(F32)], axis=0).astype(BF16)
        feat[index, 0:16, :] = jnp.concatenate([first, load(1) * scale], axis=0).astype(BF16)
        for k in range(1, 8):
            feat[index, 16 * k : 16 * k + 16, :] = jnp.concatenate([load(2 * k) * scale, load(2 * k + 1) * scale], axis=0).astype(BF16)

    def local_feat(i):
        for k in range(4):
            n = i * 4 + k
            features(cells, n, n // cols + 2, n % cols + 2)

    loop(own // 4, local_feat)

    def a_feat(i):
        for k in range(2):
            n = i * 2 + k
            features(a_low, n, jnp.int32(1), n + 2)
            features(a_high, n, jnp.int32(rows + 2), n + 2)

    loop(cols // 2, a_feat)

    def z_feat(i):
        features(z_low, i, i + 2, jnp.int32(1))
        features(z_high, i, i + 2, jnp.int32(cols + 2))

    loop(rows, z_feat)
    for n, r in enumerate((1, rows + 2)):
        features(corner_low, n, jnp.int32(r), jnp.int32(1))
        features(corner_high, n, jnp.int32(r), jnp.int32(cols + 2))

    def force(n):
        r, c, index, partners = own_cell(n)
        lhs = jnp.concatenate([feat[partner] for partner in partners], axis=1)
        sums = jnp.dot(lhs, squares[n], preferred_element_type=F32)
        g = cells[n, 0:8, :]
        m, nu = rows_of(g[6:7], 8), rows_of(g[7:8], 8)
        alive = jnp.where(m > 0.0, time_step, 0.0)
        first = sums[0:8]
        press = sums[128:136] + sums[136:144]
        press = press - positions(g, r + 2, c + 2) * jnp.where(sub8 < 4, rows_of(press[0:1], 8), rows_of(press[4:5], 8))
        press = press * jnp.where(sub8 < 4, row8(ratio, index), 1.0)
        press = press + pltpu.roll(press, 4, 0)
        weight, friction = rows_of(first[6:7], 8), rows_of(first[7:8], 8)
        surface = jnp.where(sub8 == 3, surf[n * 4], jnp.where(sub8 == 4, surf[n * 4 + 1], surf[n * 4 + 2]))
        wall = wall_gain * jnp.maximum(1.0 - 3.0 * rows_of(g[2:3], 8), 0.0)
        accel = nu * (first - g * weight) + pltpu.roll(first, 3, 0) - g * friction + wall * (surface - g)
        accel = accel - 6.0 * pltpu.roll(press, 2, 0)
        velocity = g + accel * alive
        position = g + time_step * pltpu.roll(velocity, 5, 0)
        out[n, 0:8, :] = jnp.where(sub8 < 3, position, jnp.where(sub8 < 6, velocity, g))
        gain = 2.0 * alive
        stay = 1.0 - gain * weight
        for k in range(1, 16):
            out[n, 8 * k : 8 * k + 8, :] = cells[n, 8 * k : 8 * k + 8, :] * stay + gain * sums[8 * k : 8 * k + 8]
        if not leaving:
            dens[pl.ds(n, 1), :] = jnp.where(m > 0.0, row8(rho, index), 0.0)[0:1]

    def forces(i):
        for k in range(8):
            force(i * 8 + k)

    loop(own // 8, forces)
    if leaving:
        take_out(out, slots, buffer_row, sent, gathered)


def take_out(state, slots, buffer_row, sent, gathered):
    leaving, places = slots.shape[0], sent.shape[0]
    offset = jnp.broadcast_to(slots[...], (leaving, 128)) - lax.broadcasted_iota(I32, (leaving, 128), 1)
    gathered[...] = jnp.zeros_like(gathered)
    per = 4

    def body(i):
        hits, pieces = [], []
        for k in range(per):
            c = i * per + k
            hit = jnp.where(offset == c * 128, 1.0, 0.0)
            gone = jnp.sum(hit, axis=0, keepdims=True)
            whole = state[c]
            hi, lo = halves(whole)
            hits.append(hit.astype(BF16))
            pieces.append(jnp.concatenate([hi, lo], axis=0))
            state[c] = whole * (1.0 - gone)
        gathered[...] += lax.dot_general(jnp.concatenate(hits, axis=1), jnp.concatenate(pieces, axis=1), (((1,), (1,)), ((), ())), preferred_element_type=F32)

    loop(state.shape[0] // per, body)
    place = jnp.where(jnp.broadcast_to(buffer_row[...], (places, leaving)) == sub_iota((places, leaving)), 1.0, 0.0).astype(BF16)
    right = jnp.concatenate([gathered[...].astype(BF16), jnp.ones((leaving, 128), BF16)], axis=1)
    sums = jnp.dot(place, right, preferred_element_type=F32)
    lane = lax.broadcasted_iota(I32, (places, 128), 1)
    sent[...] = jnp.where((lane == 6) & (sums[:, 256:384] < 0.5), -1.0, sums[:, 0:128] + sums[:, 128:256])


def smem_spec():
    return pl.BlockSpec(memory_space=pltpu.SMEM)


def vmem_spec():
    return pl.BlockSpec(memory_space=pltpu.VMEM)


def step_call(rows, cols, codes, surface, cells, halo, leave=None):
    own = rows * cols
    patch = (rows + 4) * (cols + 4)
    ring = 2 * (rows + 2) + 2 * cols
    new = jax.ShapeDtypeStruct((own, 128, 128), F32)
    extra = []
    if leave:
        slots, buffer_row, places = leave
        outs = (new, jax.ShapeDtypeStruct((places, 128), F32))
        extra, first = [slots, buffer_row], [pltpu.VMEM((slots.shape[0], 256), F32)]
    else:
        outs, first = (new, jax.ShapeDtypeStruct((own, 128), F32)), []
    return pl.pallas_call(
        functools.partial(step_kernel, rows, cols, bool(leave)),
        out_shape=outs,
        in_specs=[smem_spec(), smem_spec()] + [vmem_spec()] * (7 + len(extra)),
        out_specs=(vmem_spec(), vmem_spec()),
        scratch_shapes=first
        + [
            pltpu.VMEM((patch, 128, 128), BF16),
            pltpu.VMEM((patch, 32, 128), BF16),
            pltpu.VMEM((patch, 144, 128), BF16),
            pltpu.VMEM((own, 768, 128), BF16),
            pltpu.VMEM((patch * ROWS_K, 128), F32),
            pltpu.VMEM((patch * ROWS_K, 128), F32),
        ]
        + [pltpu.VMEM((patch, 128), F32)] * 5
        + [pltpu.SMEM((ring, 128), F32), pltpu.SemaphoreType.DMA((6,))],
        compiler_params=pltpu.CompilerParams(vmem_limit_bytes=60 * MIB),
    )(codes, surface, cells, *halo, *extra)


def put_strips(state, rows, cols, codes, strips):
    a_up, a_down, z_up, z_down = strips
    lane = lax.broadcasted_iota(I32, (8, 128), 1)
    sub8 = sub_iota((8, 128))

    def coded(behind, r, c):
        listed = jnp.zeros((8, 128), F32)
        for j in range(6):
            listed = jnp.where(lane == j, codes[r, c, j].astype(F32), listed)
        return jnp.where(sub8 == 7, listed, behind)

    def along(n):
        for strip, first, second in ((a_up, rows - 1, rows - 2), (a_down, 0, 1)):
            strip[n, 0:128, :] = state(first * cols + n, 128)
            strip[n, 128:136, :] = coded(state(second * cols + n, 8), first, n)

    loop(cols, along)

    def across(n):
        for strip, first, second in ((z_up, cols - 1, cols - 2), (z_down, 0, 1)):
            strip[n, 0:128, :] = state(n * cols + first, 128)
            strip[n, 128:136, :] = coded(state(n * cols + second, 8), n, first)

    loop(rows, across)


def strip_shapes(rows, cols):
    return tuple(jax.ShapeDtypeStruct((n, 136, 128), F32) for n in (cols, cols, rows, rows))


def mask_kernel(rows, cols, counts, codes, state, *strips):
    def cell(n, height):
        held = lax.broadcasted_iota(I32, (height, 128), 1) < counts[n // cols, n % cols]
        return jnp.where(held, state[n, 0:height, :], 0.0)

    put_strips(cell, rows, cols, codes, strips)


def mask_strips(rows, cols, counts, codes, state):
    return pl.pallas_call(
        functools.partial(mask_kernel, rows, cols),
        out_shape=strip_shapes(rows, cols),
        in_specs=[smem_spec(), smem_spec(), vmem_spec()],
        out_specs=(vmem_spec(),) * 4,
        compiler_params=pltpu.CompilerParams(vmem_limit_bytes=40 * MIB),
    )(counts, codes, state)


def insert_kernel(rows, cols, codes, state, incoming, slots, out, *strips):
    places = slots.shape[0]
    data = incoming[...]
    absent = jnp.broadcast_to(data[:, 6:7], (places, 128)) < 0.0
    offset = jnp.broadcast_to(slots[...], (places, 128)) - lax.broadcasted_iota(I32, (places, 128), 1)
    offset = jnp.where(absent, -1, offset)
    hi, lo = halves(jnp.transpose(data))
    left = jnp.concatenate([hi, lo, jnp.ones((16, places), BF16)], axis=0)
    per = 4

    def body(i):
        for pair in range(per // 2):
            first = i * per + pair * 2
            hits = [jnp.where(offset == (first + k) * 128, 1.0, 0.0).astype(BF16) for k in range(2)]
            sums = jnp.dot(left, jnp.concatenate(hits, axis=1), preferred_element_type=F32)
            for k in range(2):
                part = sums[:, 128 * k : 128 * (k + 1)]
                out[first + k] = state[first + k] * (1.0 - part[256:257]) + (part[0:128] + part[128:256])

    loop(rows * cols // per, body)
    put_strips(lambda n, height: out[n, 0:height, :], rows, cols, codes, strips)


def insert(rows, cols, codes, state, incoming, slots):
    return pl.pallas_call(
        functools.partial(insert_kernel, rows, cols),
        out_shape=(jax.ShapeDtypeStruct(state.shape, F32),) + strip_shapes(rows, cols),
        in_specs=[smem_spec()] + [vmem_spec()] * 3,
        out_specs=(vmem_spec(),) * 5,
        compiler_params=pltpu.CompilerParams(vmem_limit_bytes=48 * MIB),
    )(codes, state, incoming, slots)


def exchange(strips):
    n_ax, n_az = lax.axis_size("ax"), lax.axis_size("az")
    a_up, a_down, z_up, z_down = strips
    up = [(i, i + 1) for i in range(n_ax - 1)]
    around = [(i, (i + 1) % n_az) for i in range(n_az)]
    a_low = lax.ppermute(a_up, "ax", up)
    a_high = lax.ppermute(a_down, "ax", [(j, i) for i, j in up])
    z_low = lax.ppermute(z_up, "az", around)
    z_high = lax.ppermute(z_down, "az", [(j, i) for i, j in around])

    def corner(end, behind):
        return jnp.stack([jnp.concatenate([x[end], x[behind, 0:8], x[behind, 128:136]], axis=0) for x in (a_low, a_high)])

    corner_low = lax.ppermute(corner(-1, -2), "az", around)
    corner_high = lax.ppermute(corner(0, 1), "az", [(j, i) for i, j in around])
    return a_low, a_high, z_low, z_high, corner_low, corner_high


def local(particles, counts, pair_codes, contact, twist_state, leaving_slot, leaving_dest, arrival_slot):
    rows, cols, fields, block = particles.shape
    ranks = lax.axis_size("ax") * lax.axis_size("az")
    own = rows * cols

    flat = particles.reshape(own, fields, block)
    halo = exchange(mask_strips(rows, cols, counts, pair_codes, flat))

    segments = twist_state.shape[0]
    told = jnp.broadcast_to(twist_state.reshape(1, segments * 3), (ranks, segments * 3))
    twist = lax.all_to_all(told, AXES, 0, 0, tiled=True).reshape(ranks * segments, 3)
    surface = jnp.pad(twist[contact.reshape(own)], ((0, 0), (0, 1))).reshape(-1)

    dest = leaving_dest[:, 0]
    leaving = dest.shape[0]
    same = dest[:, None] == dest[None, :]
    earlier = lax.broadcasted_iota(I32, (leaving, leaving), 0) > lax.broadcasted_iota(I32, (leaving, leaving), 1)
    order = jnp.sum((same & earlier).astype(I32), axis=1)
    capacity = arrival_slot.shape[0] // ranks
    buffer_row = (dest * capacity + order).reshape(1, leaving)

    keep = lax.broadcasted_iota(I32, (own, block), 1) < counts.reshape(own, 1)
    state = jnp.where(keep[:, None, :], flat, 0.0)
    state, outgoing = step_call(rows, cols, pair_codes, surface, state, halo, (leaving_slot.reshape(-1, 1), buffer_row, ranks * capacity))
    incoming = lax.all_to_all(outgoing.reshape(ranks, capacity, fields), AXES, 0, 0, tiled=True)
    state, *strips = insert(rows, cols, pair_codes, state, incoming.reshape(-1, fields), arrival_slot.reshape(-1, 1))
    state, density = step_call(rows, cols, pair_codes, surface, state, exchange(strips))
    return state.reshape(particles.shape), density.reshape(rows, cols, block)


def solution(mesh):
    both = P("ax", "az")
    flat = P(AXES)
    return jax.shard_map(
        local,
        mesh=mesh,
        in_specs=(P("ax", "az", None, None), both, P("ax", "az", None), both, P(AXES, None), flat, P(AXES, None), flat),
        out_specs=(P("ax", "az", None, None), P("ax", "az", None)),
        check_vma=False,
    )
```

```python
import functools

import jax
import jax.numpy as jnp
from jax import lax
from jax.experimental import pallas as pl
from jax.experimental.pallas import tpu as pltpu
from jax.sharding import PartitionSpec as P

AXES = ("ax", "az")
F32, BF16, I32 = jnp.float32, jnp.bfloat16, jnp.int32

wall_gain = 4.0
time_step = 0.05
MIB = 1 << 20


def rows_of(x, n):
    return jnp.broadcast_to(x, (n,) + x.shape[1:])


def sub_iota(shape):
    return lax.broadcasted_iota(I32, shape, 0)


def halves(x):
    hi = x.astype(BF16)
    return hi, (x - hi.astype(F32)).astype(BF16)


def thirds(x):
    hi = x.astype(BF16).astype(F32)
    rest = x - hi
    mid = rest.astype(BF16).astype(F32)
    return hi, mid, rest - mid


def loop(n, body):
    def step(i, carry):
        body(i)
        return carry

    lax.fori_loop(0, n, step, 0)


ROWS_K = 32
EDGE, CORNER = 136, 152


def live_rows(g, count):
    dead = (sub_iota((8, 128)) == 6) & (lax.broadcasted_iota(I32, (8, 128), 1) >= count)
    return jnp.where(dead, 0.0, g)


def with_codes(behind, codes, r, c):
    lane = lax.broadcasted_iota(I32, (8, 128), 1)
    listed = jnp.zeros((8, 128), F32)
    for j in range(6):
        listed = jnp.where(lane == j, codes[r, c, j].astype(F32), listed)
    return jnp.where(sub_iota((8, 128)) == 7, listed, behind)


def pieces(source, target, semaphore, per):
    def piece(i):
        part = pl.ds(i * per, per)
        return pltpu.make_async_copy(source.at[part], target.at[part], semaphore.at[i])

    return piece


def smem_spec():
    return pl.BlockSpec(memory_space=pltpu.SMEM)


def vmem_spec():
    return pl.BlockSpec(memory_space=pltpu.VMEM)


def any_spec():
    return pl.BlockSpec(memory_space=pl.ANY)


FULL = pltpu.CompilerParams(vmem_limit_bytes=60 * MIB)


def strip_shapes(rows, cols):
    entries = ((2, CORNER), (2, CORNER), (cols, EDGE), (cols, EDGE), (rows, EDGE), (rows, EDGE))
    return tuple(jax.ShapeDtypeStruct((n, height, 128), F32) for n, height in entries)


def put_strips(rows, cols, codes, geo, strips):
    ends_up, ends_down, a_up, a_down, z_up, z_down = strips
    sides = ((ends_up, a_up, rows - 1, rows - 2), (ends_down, a_down, 0, 1))

    def along(i):
        for k in range(4):
            n = i * 4 + k
            for _, strip, first, second in sides:
                strip[n, 0:8, :] = geo(first, n)
                strip[n, 128:136, :] = with_codes(geo(second, n), codes, first, n)

    loop(cols // 4, along)
    for strip, first, second in ((z_up, cols - 1, cols - 2), (z_down, 0, 1)):
        for r in range(rows):
            strip[r, 0:8, :] = geo(r, first)
            strip[r, 128:136, :] = with_codes(geo(r, second), codes, r, first)
    for strip, _, first, second in sides:
        for n, (near, far) in enumerate(((0, 1), (cols - 1, cols - 2))):
            strip[n, 0:8, :] = geo(first, near)
            strip[n, 128:136, :] = with_codes(geo(second, near), codes, first, near)
            strip[n, 136:144, :] = geo(first, far)
            strip[n, 144:152, :] = geo(second, far)


def fill_strips(rows, cols, state, strips, semaphore):
    ends_up, ends_down, a_up, a_down, z_up, z_down = strips
    parts = []
    for ends, strip, r in ((ends_up, a_up, rows - 1), (ends_down, a_down, 0)):
        parts.append((state.at[pl.ds(r * cols, cols), 8:128, :], strip.at[:, 8:128, :]))
        for n, c in enumerate((0, cols - 1)):
            parts.append((state.at[r * cols + c, 8:128, :], ends.at[n, 8:128, :]))
    for strip, c in ((z_up, cols - 1), (z_down, 0)):
        for r in range(rows):
            parts.append((state.at[r * cols + c, 8:128, :], strip.at[r, 8:128, :]))
    return [pltpu.make_async_copy(a, b, semaphore.at[k]) for k, (a, b) in enumerate(parts)]


def mask_kernel(rows, cols, counts, codes, state, *refs):
    strips, (rows8, came, semaphore) = refs[:6], refs[6:]
    first = pltpu.make_async_copy(state.at[:, 0:8, :], rows8, came)
    first.start()
    copies = fill_strips(rows, cols, state, strips, semaphore)
    for copy in copies:
        copy.start()
    first.wait()
    put_strips(rows, cols, codes, lambda r, c: live_rows(rows8[r * cols + c], counts[r, c]), strips)
    for copy in copies:
        copy.wait()


def mask_strips(rows, cols, counts, codes, state):
    return pl.pallas_call(
        functools.partial(mask_kernel, rows, cols),
        out_shape=strip_shapes(rows, cols),
        in_specs=[smem_spec(), smem_spec(), any_spec()],
        out_specs=(vmem_spec(),) * 6,
        scratch_shapes=[pltpu.VMEM((rows * cols, 8, 128), F32), pltpu.SemaphoreType.DMA(()), pltpu.SemaphoreType.DMA((6 + 2 * rows,))],
        compiler_params=FULL,
    )(counts, codes, state)


def linked(center, code, width):
    up = (code * 11) >> 5
    return center + up * (width - 3) + code - (width + 1)


def step_kernel(rows, cols, masked, leaving, *refs):
    if masked:
        counts, refs = refs[0], refs[1:]
    codes, surf, cells_in, a_low, a_high, z_low, z_high = refs[:7]
    if leaving:
        slots, buffer_row, out_ref, sent, gathered = refs[7:12]
        refs = refs[12:]
    else:
        out_ref, dens = refs[7:9]
        refs = refs[9:]
    geo, cells, out, side_t, side_s, feat, squares, row_t, row_s = refs[:9]
    mass, root, rho, ratio, inverse, ring_codes, geo_came, cells_came, out_left, codes_came = refs[9:]
    width = cols + 4
    own = rows * cols
    z_rows = rows * EDGE
    sub8 = sub_iota((8, 128))
    row_mid, col_mid = (rows + 3) / 2.0, (cols + 3) / 2.0

    geo_copy = pltpu.make_async_copy(cells_in.at[:, 0:8, :], geo, geo_came)
    geo_copy.start()
    code_copies = []

    def bring_codes(source, first, n):
        code_copies.append(pltpu.make_async_copy(source, ring_codes.at[pl.ds(first, n), :], codes_came.at[len(code_copies)]))

    bring_codes(a_low.at[:, EDGE - 1, :], 0, cols)
    bring_codes(a_high.at[:, EDGE - 1, :], cols, cols)
    for ref, first in ((z_low, 2 * cols), (z_high, 2 * cols + rows + 2)):
        for r in range(rows):
            bring_codes(ref.at[pl.ds(r * EDGE + EDGE - 1, 1), :], first + r, 1)
        for n in range(2):
            bring_codes(ref.at[pl.ds(z_rows + n * CORNER + EDGE - 1, 1), :], first + rows + n, 1)
    cells_piece = pieces(cells_in, cells, cells_came, 8)
    out_piece = pieces(out, out_ref, out_left, 8)
    for copy in code_copies:
        copy.start()
    for i in range(own // 8):
        cells_piece(i).start()

    def geometry(flat, row, stride, n, index, apart, r, c, center, limit=None):
        def field(k):
            return flat[pl.ds(row + k, n, stride=stride), :]

        x = [field(0) + (r - row_mid), field(1) + (c - col_mid), field(2)]
        norm = x[0] * x[0] + x[1] * x[1] + x[2] * x[2]
        m = field(6)
        if limit is not None:
            m = jnp.where(lax.broadcasted_iota(I32, (n, 128), 1) < limit, m, 0.0)
        cube = jnp.exp2(jnp.log2(jnp.maximum(m, 1e-30)) * (1.0 / 3.0))
        cube = cube - (cube - m / (cube * cube)) * (1.0 / 3.0)
        cube = jnp.where(m > 0.0, cube, 0.0)

        def put(target, k, value):
            target[pl.ds(index * ROWS_K + k, n, stride=apart * ROWS_K), :] = value

        for k, value in enumerate([x[0] * cube, x[1] * cube, x[2] * cube, -norm * cube, cube]):
            hi, mid, low = thirds(value)
            for block, piece in enumerate((hi, mid, low, hi, mid, hi)):
                put(row_t, 5 * block + k, piece)
        put(row_t, 30, jnp.zeros_like(m))
        put(row_t, 31, jnp.zeros_like(m))
        for k in range(n):
            mass[pl.ds(index + k * apart, 1), :] = m[k : k + 1]
            root[pl.ds(index + k * apart, 1), :] = cube[k : k + 1]
        if center:
            for k, value in enumerate([x[0] + x[0], x[1] + x[1], x[2] + x[2], jnp.ones_like(m), 1.0 - norm]):
                hi, mid, low = thirds(value)
                for block, piece in enumerate((hi, hi, hi, mid, mid, low)):
                    put(row_s, 5 * block + k, piece)
            put(row_s, 30, jnp.zeros_like(m))
            put(row_s, 31, jnp.zeros_like(m))

    def sub(n):
        return sub_iota((n, 128)).astype(F32)

    per = 8
    geo_copy.wait()
    geo_flat = geo.reshape(own * 8, 128)

    def local_geo(i):
        first = i * per
        r, c = first // cols + 2, first % cols + 2
        limit = None
        if masked:
            limit = jnp.zeros((per, 128), I32)
            for k in range(per):
                limit = jnp.where(sub_iota((per, 128)) == k, counts[first // cols, first % cols + k], limit)
        geometry(geo_flat, first * 8, 8, per, r * width + c, 1, r.astype(F32), c.astype(F32) + sub(per), True, limit)

    loop(own // per, local_geo)
    for ref, first, second in ((a_low, 1, 0), (a_high, rows + 2, rows + 3)):
        flat = ref.reshape(cols * EDGE, 128)
        for k in range(0, cols, per):
            c = k + 2.0 + sub(per)
            geometry(flat, k * EDGE, EDGE, per, first * width + k + 2, 1, float(first), c, True)
            geometry(flat, k * EDGE + 128, EDGE, per, second * width + k + 2, 1, float(second), c, False)
    for ref, near, far in ((z_low, 1, 0), (z_high, cols + 2, cols + 3)):
        r = 2.0 + sub(rows)
        geometry(ref, 0, EDGE, rows, 2 * width + near, width, r, float(near), True)
        geometry(ref, 128, EDGE, rows, 2 * width + far, width, r, float(far), False)
        apart = (rows + 1) * width
        r = 1.0 + (rows + 1.0) * sub(2)
        geometry(ref, z_rows, CORNER, 2, width + near, apart, r, float(near), True)
        geometry(ref, z_rows + 136, CORNER, 2, width + far, apart, r, float(far), False)
        apart = (rows + 3) * width
        r = (rows + 3.0) * sub(2)
        geometry(ref, z_rows + 128, CORNER, 2, near, apart, r, float(near), False)
        geometry(ref, z_rows + 144, CORNER, 2, far, apart, r, float(far), False)

    quarter = lax.broadcasted_iota(I32, (128, 128), 1) // ROWS_K
    only = [jnp.where(quarter == k, 1.0, 0.0).astype(BF16) for k in range(4)]

    def block32(ref, index):
        return ref[pl.ds(pl.multiple_of(index * ROWS_K, ROWS_K), ROWS_K), :]

    def turn(indices):
        t = jnp.transpose(jnp.concatenate([block32(row_t, index) for index in indices], axis=0)).astype(BF16)
        for k, index in enumerate(indices):
            side_t[index] = t * only[k]
            side_s[index] = block32(row_s, index).astype(BF16)

    def turn_own(i):
        for k in range(cols // 4):
            index = (i + 2) * width + 2 + 4 * k
            turn([index, index + 1, index + 2, index + 3])

    loop(rows, turn_own)

    def turn_ring(i):
        for r in (i, i + rows + 2):
            for k in range(width // 4):
                index = r * width + 4 * k
                turn([index, index + 1, index + 2, index + 3])
        for r in (2 * i + 2, 2 * i + 3):
            turn([r * width, r * width + 1, r * width + cols + 2, r * width + cols + 3])

    loop(2, turn_ring)

    def density(center, partners, n):
        rhs = jnp.concatenate([side_s[center]] * 4, axis=0)
        total = jnp.zeros((8, 128), F32)
        for j, partner in enumerate(partners):
            y = jnp.maximum(jnp.dot(side_t[partner], rhs, preferred_element_type=F32), 0.0)
            square = y * y
            total = total + jnp.sum((square * y).reshape(16, 8, 128), axis=0)
            if n is not None:
                squares[n, j * 128 : (j + 1) * 128, :] = square.astype(BF16)
        rho[pl.ds(center, 1), :] = jnp.sum(total, axis=0, keepdims=True)

    rho[...] = jnp.ones_like(rho)

    def own_density(i):
        for k in range(8):
            n = i * 8 + k
            r, c = n // cols, n % cols
            center = (r + 2) * width + c + 2
            density(center, [linked(center, codes[r, c, j], width) for j in range(6)], n)

    loop(own // 8, own_density)
    for copy in code_copies:
        copy.wait()

    def ring_cell(center, n):
        density(center, [linked(center, ring_codes[n, j].astype(I32), width) for j in range(6)], None)

    def ring_rows(i):
        for k in range(4):
            c = i * 4 + k
            ring_cell(width + c + 2, c)
            ring_cell((rows + 2) * width + c + 2, cols + c)

    loop(cols // 4, ring_rows)
    for k, r in enumerate([r + 2 for r in range(rows)] + [1, rows + 2]):
        ring_cell(r * width + 1, 2 * cols + k)
        ring_cell(r * width + cols + 2, 2 * cols + rows + 2 + k)

    living = mass[...] > 0.0
    guarded = jnp.where(living, rho[...], 1.0)
    ratio[...] = jnp.where(living, (guarded - 1.0) / (guarded * guarded), 0.0)
    inverse[...] = jnp.where(living, 1.0 / guarded, 0.0)

    def row8(ref, index):
        return rows_of(ref[pl.ds(index, 1), :], 8)

    def shifted(g, r, c):
        off_r = r.astype(F32) - row_mid
        off_c = c.astype(F32) - col_mid
        return jnp.where(sub8 == 0, g + off_r, jnp.where(sub8 == 1, g + off_c, g))

    def positions(g, r, c):
        x = shifted(g, r, c)
        return jnp.where((sub8 == 0) | (sub8 == 4), 1.0, jnp.where(sub8 < 4, pltpu.roll(x, 1, 0), pltpu.roll(x, 5, 0)))

    def features(load, r, c):
        index = r * width + c
        cube = row8(root, index)
        scale = cube * row8(inverse, index)

        g = load(0)
        nu = rows_of(g[7:8], 8)
        first = jnp.where(sub8 < 3, pltpu.roll(g, 5, 0) * nu, jnp.where(sub8 == 6, 1.0, g)) * scale
        press = positions(g, r, c) * jnp.where(sub8 < 4, cube, cube * row8(ratio, index))
        hi, lo = halves(press)
        feat[index, 128:144, :] = jnp.concatenate([hi.astype(F32), lo.astype(F32)], axis=0).astype(BF16)
        feat[index, 0:16, :] = jnp.concatenate([first, load(1) * scale], axis=0).astype(BF16)
        for k in range(1, 8):
            feat[index, 16 * k : 16 * k + 16, :] = jnp.concatenate([load(2 * k) * scale, load(2 * k + 1) * scale], axis=0).astype(BF16)

    def in_cell(ref, n):
        return lambda k: ref[n, 8 * k : 8 * k + 8, :]

    def in_rows(ref, row):
        return lambda k: ref[row + 8 * k : row + 8 * k + 8, :]

    def local_feat(i):
        cells_piece(i).wait()
        for k in range(8):
            n = i * 8 + k
            features(in_cell(cells, n), n // cols + 2, n % cols + 2)

    loop(own // 8, local_feat)

    def a_feat(i):
        for k in range(4):
            n = i * 4 + k
            features(in_cell(a_low, n), jnp.int32(1), n + 2)
            features(in_cell(a_high, n), jnp.int32(rows + 2), n + 2)

    loop(cols // 4, a_feat)
    for ref, c in ((z_low, 1), (z_high, cols + 2)):
        for r in range(rows):
            features(in_rows(ref, r * EDGE), jnp.int32(r + 2), jnp.int32(c))
        for n, r in enumerate((1, rows + 2)):
            features(in_rows(ref, z_rows + n * CORNER), jnp.int32(r), jnp.int32(c))

    def force(n):
        r, c = n // cols, n % cols
        index = (r + 2) * width + c + 2
        lhs = jnp.concatenate([feat[linked(index, codes[r, c, j], width)] for j in range(6)], axis=1)
        sums = jnp.dot(lhs, squares[n], preferred_element_type=F32)
        if masked:
            held = lax.broadcasted_iota(I32, (8, 128), 1) < counts[r, c]

        def load(k):
            value = cells[n, 8 * k : 8 * k + 8, :]
            return jnp.where(held, value, 0.0) if masked else value

        g = load(0)
        m, nu = rows_of(g[6:7], 8), rows_of(g[7:8], 8)
        alive = jnp.where(m > 0.0, time_step, 0.0)
        first = sums[0:8]
        press = sums[128:136] + sums[136:144]
        press = press - positions(g, r + 2, c + 2) * jnp.where(sub8 < 4, rows_of(press[0:1], 8), rows_of(press[4:5], 8))
        press = press * jnp.where(sub8 < 4, row8(ratio, index), 1.0)
        press = press + pltpu.roll(press, 4, 0)
        weight, friction = rows_of(first[6:7], 8), rows_of(first[7:8], 8)
        surface = jnp.where(sub8 == 3, surf[n * 4], jnp.where(sub8 == 4, surf[n * 4 + 1], surf[n * 4 + 2]))
        wall = wall_gain * jnp.maximum(1.0 - 3.0 * rows_of(g[2:3], 8), 0.0)
        accel = nu * (first - g * weight) + pltpu.roll(first, 3, 0) - g * friction + wall * (surface - g)
        accel = accel - 6.0 * pltpu.roll(press, 2, 0)
        velocity = g + accel * alive
        position = g + time_step * pltpu.roll(velocity, 5, 0)
        out[n, 0:8, :] = jnp.where(sub8 < 3, position, jnp.where(sub8 < 6, velocity, g))
        gain = 2.0 * alive
        stay = 1.0 - gain * weight
        for k in range(1, 16):
            out[n, 8 * k : 8 * k + 8, :] = load(k) * stay + gain * sums[8 * k : 8 * k + 8]
        if not leaving:
            dens[pl.ds(n, 1), :] = jnp.where(m > 0.0, row8(rho, index), 0.0)[0:1]

    def forces(i):
        for k in range(8):
            force(i * 8 + k)
        if not leaving:
            out_piece(i).start()

    loop(own // 8, forces)
    if leaving:
        take_out(out, slots, buffer_row, sent, gathered, out_piece)
    for i in range(own // 8):
        out_piece(i).wait()


def take_out(state, slots, buffer_row, sent, gathered, out_piece):
    leaving, places = slots.shape[0], sent.shape[0]
    offset = jnp.broadcast_to(slots[...], (leaving, 128)) - lax.broadcasted_iota(I32, (leaving, 128), 1)
    gathered[...] = jnp.zeros_like(gathered)
    per = 8

    def body(i):
        hits, parts = [], []
        for k in range(per):
            c = i * per + k
            hit = jnp.where(offset == c * 128, 1.0, 0.0)
            gone = jnp.sum(hit, axis=0, keepdims=True)
            whole = state[c]
            hi, lo = halves(whole)
            hits.append(hit.astype(BF16))
            parts.append(jnp.concatenate([hi, lo], axis=0))
            state[c] = whole * (1.0 - gone)
        gathered[...] += lax.dot_general(jnp.concatenate(hits, axis=1), jnp.concatenate(parts, axis=1), (((1,), (1,)), ((), ())), preferred_element_type=F32)
        out_piece(i).start()

    loop(state.shape[0] // per, body)
    place = jnp.where(jnp.broadcast_to(buffer_row[...], (places, leaving)) == sub_iota((places, leaving)), 1.0, 0.0).astype(BF16)
    right = jnp.concatenate([gathered[...].astype(BF16), jnp.ones((leaving, 128), BF16)], axis=1)
    sums = jnp.dot(place, right, preferred_element_type=F32)
    lane = lax.broadcasted_iota(I32, (places, 128), 1)
    sent[...] = jnp.where((lane == 6) & (sums[:, 256:384] < 0.5), -1.0, sums[:, 0:128] + sums[:, 128:256])


def smem_spec():
    return pl.BlockSpec(memory_space=pltpu.SMEM)


def vmem_spec():
    return pl.BlockSpec(memory_space=pltpu.VMEM)


def step_call(rows, cols, counts, codes, surface, cells, halo, leave=None):
    own = rows * cols
    patch = (rows + 4) * (cols + 4)
    ring = 2 * cols + 2 * (rows + 2)
    new = jax.ShapeDtypeStruct((own, 128, 128), F32)
    extra, first = [], []
    if leave:
        slots, buffer_row, places = leave
        outs = (new, jax.ShapeDtypeStruct((places, 128), F32))
        extra, first = [slots, buffer_row], [pltpu.VMEM((slots.shape[0], 256), F32)]
    else:
        outs = (new, jax.ShapeDtypeStruct((own, 128), F32))
    scalars = [] if counts is None else [counts]
    return pl.pallas_call(
        functools.partial(step_kernel, rows, cols, counts is not None, bool(leave)),
        out_shape=outs,
        in_specs=[smem_spec()] * (len(scalars) + 2) + [any_spec()] + [vmem_spec()] * (4 + len(extra)),
        out_specs=(any_spec(), vmem_spec()),
        scratch_shapes=first
        + [
            pltpu.VMEM((own, 8, 128), F32),
            pltpu.VMEM((own, 128, 128), F32),
            pltpu.VMEM((own, 128, 128), F32),
            pltpu.VMEM((patch, 128, 128), BF16),
            pltpu.VMEM((patch, 32, 128), BF16),
            pltpu.VMEM((patch, 144, 128), BF16),
            pltpu.VMEM((own, 768, 128), BF16),
            pltpu.VMEM((patch * ROWS_K, 128), F32),
            pltpu.VMEM((patch * ROWS_K, 128), F32),
        ]
        + [pltpu.VMEM((patch, 128), F32)] * 5
        + [
            pltpu.SMEM((ring, 128), F32),
            pltpu.SemaphoreType.DMA(()),
            pltpu.SemaphoreType.DMA((own // 8,)),
            pltpu.SemaphoreType.DMA((own // 8,)),
            pltpu.SemaphoreType.DMA((2 + 2 * (rows + 2),)),
        ],
        compiler_params=pltpu.CompilerParams(vmem_limit_bytes=52 * MIB),
    )(*scalars, codes, surface, cells, *halo, *extra)


def insert_kernel(rows, cols, codes, state_in, incoming, slots, out_ref, *refs):
    strips, (state, out, came, left_for, semaphore) = refs[:6], refs[6:]
    arrive = pieces(state_in, state, came, 8)
    leave = pieces(out, out_ref, left_for, 8)
    for i in range(rows * cols // 8):
        arrive(i).start()
    places = slots.shape[0]
    data = incoming[...]
    absent = jnp.broadcast_to(data[:, 6:7], (places, 128)) < 0.0
    offset = jnp.broadcast_to(slots[...], (places, 128)) - lax.broadcasted_iota(I32, (places, 128), 1)
    offset = jnp.where(absent, -1, offset)
    hi, lo = halves(jnp.transpose(data))
    left = jnp.concatenate([hi, lo, jnp.ones((16, places), BF16)], axis=0)
    per = 8

    def body(i):
        arrive(i).wait()
        for pair in range(per // 2):
            first = i * per + pair * 2
            hits = [jnp.where(offset == (first + k) * 128, 1.0, 0.0).astype(BF16) for k in range(2)]
            sums = jnp.dot(left, jnp.concatenate(hits, axis=1), preferred_element_type=F32)
            for k in range(2):
                part = sums[:, 128 * k : 128 * (k + 1)]
                out[first + k] = state[first + k] * (1.0 - part[256:257]) + (part[0:128] + part[128:256])
        leave(i).start()

    loop(rows * cols // per, body)
    copies = fill_strips(rows, cols, out, strips, semaphore)
    for copy in copies:
        copy.start()
    put_strips(rows, cols, codes, lambda r, c: out[r * cols + c, 0:8, :], strips)
    for copy in copies:
        copy.wait()
    for i in range(rows * cols // per):
        leave(i).wait()


def insert(rows, cols, codes, state, incoming, slots):
    own = rows * cols
    return pl.pallas_call(
        functools.partial(insert_kernel, rows, cols),
        out_shape=(jax.ShapeDtypeStruct(state.shape, F32),) + strip_shapes(rows, cols),
        in_specs=[smem_spec(), any_spec(), vmem_spec(), vmem_spec()],
        out_specs=(any_spec(),) + (vmem_spec(),) * 6,
        scratch_shapes=[pltpu.VMEM((own, 128, 128), F32)] * 2 + [pltpu.SemaphoreType.DMA((own // 8,))] * 2 + [pltpu.SemaphoreType.DMA((6 + 2 * rows,))],
        compiler_params=pltpu.CompilerParams(vmem_limit_bytes=52 * MIB),
    )(codes, state, incoming, slots)


def swap(up, down, axis):
    n = lax.axis_size(axis)
    pairs = [(i, (i + 1) % n) for i in range(n if axis == "az" else n - 1)]
    return lax.ppermute(up, axis, pairs), lax.ppermute(down, axis, [(j, i) for i, j in pairs])


def exchange(strips):
    ends_up, ends_down, a_up, a_down, z_up, z_down = strips
    low, high = swap(ends_up, ends_down, "ax")
    a_low, a_high = swap(a_up, a_down, "ax")

    def beside(strip, n):
        return jnp.concatenate([strip.reshape(-1, 128), low[n], high[n]], axis=0)

    sides = beside(z_up, 1), beside(z_down, 0)
    return (a_low, a_high) + swap(*sides, "az"), sides


def local(particles, counts, pair_codes, contact, twist_state, leaving_slot, leaving_dest, arrival_slot):
    rows, cols, fields, block = particles.shape
    ranks = lax.axis_size("ax") * lax.axis_size("az")
    own = rows * cols
    state = particles.reshape(own, fields, block)
    halo, sides = exchange(mask_strips(rows, cols, counts, pair_codes, state))

    segments = twist_state.shape[0]
    twist_state, _ = lax.optimization_barrier((twist_state, sides))
    told = jnp.broadcast_to(twist_state.reshape(1, segments * 3), (ranks, segments * 3))
    twist = lax.all_to_all(told, AXES, 0, 0, tiled=True).reshape(ranks * segments, 3)
    surface = jnp.pad(twist[contact.reshape(own)], ((0, 0), (0, 1))).reshape(-1)

    dest = leaving_dest[:, 0]
    leaving = dest.shape[0]
    same = dest[:, None] == dest[None, :]
    earlier = lax.broadcasted_iota(I32, (leaving, leaving), 0) > lax.broadcasted_iota(I32, (leaving, leaving), 1)
    order = jnp.sum((same & earlier).astype(I32), axis=1)
    capacity = arrival_slot.shape[0] // ranks
    buffer_row = (dest * capacity + order).reshape(1, leaving)

    leave = (leaving_slot.reshape(-1, 1), buffer_row, ranks * capacity)
    state, outgoing = step_call(rows, cols, counts, pair_codes, surface, state, halo, leave)
    incoming = lax.all_to_all(outgoing.reshape(ranks, capacity, fields), AXES, 0, 0, tiled=True)
    state, *strips = insert(rows, cols, pair_codes, state, incoming.reshape(-1, fields), arrival_slot.reshape(-1, 1))
    state, density = step_call(rows, cols, None, pair_codes, surface, state, exchange(strips)[0])
    return state.reshape(particles.shape), density.reshape(rows, cols, block)


def solution(mesh):
    both = P("ax", "az")
    flat = P(AXES)
    return jax.shard_map(
        local,
        mesh=mesh,
        in_specs=(P("ax", "az", None, None), both, P("ax", "az", None), both, P(AXES, None), flat, P(AXES, None), flat),
        out_specs=(P("ax", "az", None, None), P("ax", "az", None)),
        check_vma=False,
    )
```

```python
import functools

import jax
import jax.numpy as jnp
from jax import lax
from jax.experimental import pallas as pl
from jax.experimental.pallas import tpu as pltpu
from jax.sharding import PartitionSpec as P

AXES = ("ax", "az")
F32, BF16, I32 = jnp.float32, jnp.bfloat16, jnp.int32

wall_gain = 4.0
time_step = 0.05
MIB = 1 << 20


def rows_of(x, n):
    return jnp.broadcast_to(x, (n,) + x.shape[1:])


def sub_iota(shape):
    return lax.broadcasted_iota(I32, shape, 0)


def halves(x):
    hi = x.astype(BF16)
    return hi, (x - hi.astype(F32)).astype(BF16)


def thirds(x):
    hi = x.astype(BF16).astype(F32)
    rest = x - hi
    mid = rest.astype(BF16).astype(F32)
    return hi, mid, rest - mid


def loop(n, body):
    def step(i, carry):
        body(i)
        return carry

    lax.fori_loop(0, n, step, 0)


ROWS_K = 32
EDGE, CORNER = 136, 152


def live_rows(g, count):
    dead = (sub_iota((8, 128)) == 6) & (lax.broadcasted_iota(I32, (8, 128), 1) >= count)
    return jnp.where(dead, 0.0, g)


def with_codes(behind, codes, r, c):
    lane = lax.broadcasted_iota(I32, (8, 128), 1)
    listed = jnp.zeros((8, 128), F32)
    for j in range(6):
        listed = jnp.where(lane == j, codes[j, r, c].astype(F32), listed)
    return jnp.where(sub_iota((8, 128)) == 7, listed, behind)


def pieces(source, target, semaphore, per):
    def piece(i):
        part = pl.ds(i * per, per)
        return pltpu.make_async_copy(source.at[part], target.at[part], semaphore.at[i])

    return piece


def smem_spec():
    return pl.BlockSpec(memory_space=pltpu.SMEM)


def vmem_spec():
    return pl.BlockSpec(memory_space=pltpu.VMEM)


def any_spec():
    return pl.BlockSpec(memory_space=pl.ANY)


FULL = pltpu.CompilerParams(vmem_limit_bytes=60 * MIB)


def strip_shapes(rows, cols):
    entries = ((2, CORNER), (2, CORNER), (cols, EDGE), (cols, EDGE), (rows, EDGE), (rows, EDGE))
    return tuple(jax.ShapeDtypeStruct((n, height, 128), F32) for n, height in entries)


def put_strips(rows, cols, codes, geo, strips):
    ends_up, ends_down, a_up, a_down, z_up, z_down = strips
    sides = ((ends_up, a_up, rows - 1, rows - 2), (ends_down, a_down, 0, 1))

    def along(i):
        for k in range(4):
            n = i * 4 + k
            for _, strip, first, second in sides:
                strip[n, 0:8, :] = geo(first, n)
                strip[n, 128:136, :] = with_codes(geo(second, n), codes, first, n)

    loop(cols // 4, along)
    for strip, first, second in ((z_up, cols - 1, cols - 2), (z_down, 0, 1)):
        for r in range(rows):
            strip[r, 0:8, :] = geo(r, first)
            strip[r, 128:136, :] = with_codes(geo(r, second), codes, r, first)
    for strip, _, first, second in sides:
        for n, (near, far) in enumerate(((0, 1), (cols - 1, cols - 2))):
            strip[n, 0:8, :] = geo(first, near)
            strip[n, 128:136, :] = with_codes(geo(second, near), codes, first, near)
            strip[n, 136:144, :] = geo(first, far)
            strip[n, 144:152, :] = geo(second, far)


def fill_strips(rows, cols, state, strips, semaphore):
    ends_up, ends_down, a_up, a_down, z_up, z_down = strips
    parts = []
    for ends, strip, r in ((ends_up, a_up, rows - 1), (ends_down, a_down, 0)):
        parts.append((state.at[pl.ds(r * cols, cols), 8:128, :], strip.at[:, 8:128, :]))
        for n, c in enumerate((0, cols - 1)):
            parts.append((state.at[r * cols + c, 8:128, :], ends.at[n, 8:128, :]))
    for strip, c in ((z_up, cols - 1), (z_down, 0)):
        for r in range(rows):
            parts.append((state.at[r * cols + c, 8:128, :], strip.at[r, 8:128, :]))
    return [pltpu.make_async_copy(a, b, semaphore.at[k]) for k, (a, b) in enumerate(parts)]


def mask_kernel(rows, cols, counts, codes, state, *refs):
    strips, (rows8, came, semaphore) = refs[:6], refs[6:]
    first = pltpu.make_async_copy(state.at[:, 0:8, :], rows8, came)
    first.start()
    copies = fill_strips(rows, cols, state, strips, semaphore)
    for copy in copies:
        copy.start()
    first.wait()
    put_strips(rows, cols, codes, lambda r, c: live_rows(rows8[r * cols + c], counts[r, c]), strips)
    for copy in copies:
        copy.wait()


def mask_strips(rows, cols, counts, codes, state):
    return pl.pallas_call(
        functools.partial(mask_kernel, rows, cols),
        out_shape=strip_shapes(rows, cols),
        in_specs=[smem_spec(), smem_spec(), any_spec()],
        out_specs=(vmem_spec(),) * 6,
        scratch_shapes=[pltpu.VMEM((rows * cols, 8, 128), F32), pltpu.SemaphoreType.DMA(()), pltpu.SemaphoreType.DMA((6 + 2 * rows,))],
        compiler_params=FULL,
    )(counts, codes, state)


def linked(center, code, width):
    up = (code * 11) >> 5
    return center + up * (width - 3) + code - (width + 1)


def step_kernel(rows, cols, masked, leaving, *refs):
    if masked:
        counts, refs = refs[0], refs[1:]
    codes, segments, contact, cells_in, a_low, a_high, z_low, z_high = refs[:8]
    if leaving:
        slots, buffer_row, out_ref, sent, gathered = refs[8:13]
        refs = refs[13:]
    else:
        out_ref, dens = refs[8:10]
        refs = refs[10:]
    geo, cells, out, side_t, side_s, feat, squares, row_t, row_s = refs[:9]
    mass, root, rho, ratio, inverse, ring_codes, geo_came, cells_came, out_left, codes_came = refs[9:]
    width = cols + 4
    own = rows * cols
    z_rows = rows * EDGE
    per_device = segments.shape[1] // 3
    sub8 = sub_iota((8, 128))
    row_mid, col_mid = (rows + 3) / 2.0, (cols + 3) / 2.0

    geo_copy = pltpu.make_async_copy(cells_in.at[:, 0:8, :], geo, geo_came)
    geo_copy.start()
    code_copies = []

    def bring_codes(source, first, n):
        code_copies.append(pltpu.make_async_copy(source, ring_codes.at[pl.ds(first, n), :], codes_came.at[len(code_copies)]))

    bring_codes(a_low.at[:, EDGE - 1, :], 0, cols)
    bring_codes(a_high.at[:, EDGE - 1, :], cols, cols)
    for ref, first in ((z_low, 2 * cols), (z_high, 2 * cols + rows + 2)):
        for r in range(rows):
            bring_codes(ref.at[pl.ds(r * EDGE + EDGE - 1, 1), :], first + r, 1)
        for n in range(2):
            bring_codes(ref.at[pl.ds(z_rows + n * CORNER + EDGE - 1, 1), :], first + rows + n, 1)
    cells_piece = pieces(cells_in, cells, cells_came, 8)
    out_piece = pieces(out, out_ref, out_left, 8)
    for copy in code_copies:
        copy.start()
    for i in range(own // 8):
        cells_piece(i).start()

    def geometry(flat, row, stride, n, index, apart, r, c, center, limit=None):
        def field(k):
            return flat[pl.ds(row + k, n, stride=stride), :]

        x = [field(0) + (r - row_mid), field(1) + (c - col_mid), field(2)]
        norm = x[0] * x[0] + x[1] * x[1] + x[2] * x[2]
        m = field(6)
        if limit is not None:
            m = jnp.where(lax.broadcasted_iota(I32, (n, 128), 1) < limit, m, 0.0)
        cube = jnp.exp2(jnp.log2(jnp.maximum(m, 1e-30)) * (1.0 / 3.0))
        cube = cube - (cube - m / (cube * cube)) * (1.0 / 3.0)
        cube = jnp.where(m > 0.0, cube, 0.0)

        def put(target, k, value):
            target[pl.ds(index * ROWS_K + k, n, stride=apart * ROWS_K), :] = value

        for k, value in enumerate([x[0] * cube, x[1] * cube, x[2] * cube, -norm * cube, cube]):
            hi, mid, low = thirds(value)
            for block, piece in enumerate((hi, mid, low, hi, mid, hi)):
                put(row_t, 5 * block + k, piece)
        put(row_t, 30, jnp.zeros_like(m))
        put(row_t, 31, jnp.zeros_like(m))
        for k in range(n):
            mass[pl.ds(index + k * apart, 1), :] = m[k : k + 1]
            root[pl.ds(index + k * apart, 1), :] = cube[k : k + 1]
        if center:
            for k, value in enumerate([x[0] + x[0], x[1] + x[1], x[2] + x[2], jnp.ones_like(m), 1.0 - norm]):
                hi, mid, low = thirds(value)
                for block, piece in enumerate((hi, hi, hi, mid, mid, low)):
                    put(row_s, 5 * block + k, piece)
            put(row_s, 30, jnp.zeros_like(m))
            put(row_s, 31, jnp.zeros_like(m))

    def sub(n):
        return sub_iota((n, 128)).astype(F32)

    per = 8
    geo_copy.wait()
    geo_flat = geo.reshape(own * 8, 128)

    def local_geo(i):
        first = i * per
        r, c = first // cols + 2, first % cols + 2
        limit = None
        if masked:
            limit = jnp.zeros((per, 128), I32)
            for k in range(per):
                limit = jnp.where(sub_iota((per, 128)) == k, counts[first // cols, first % cols + k], limit)
        geometry(geo_flat, first * 8, 8, per, r * width + c, 1, r.astype(F32), c.astype(F32) + sub(per), True, limit)

    loop(own // per, local_geo)
    for ref, first, second in ((a_low, 1, 0), (a_high, rows + 2, rows + 3)):
        flat = ref.reshape(cols * EDGE, 128)
        for k in range(0, cols, per):
            c = k + 2.0 + sub(per)
            geometry(flat, k * EDGE, EDGE, per, first * width + k + 2, 1, float(first), c, True)
            geometry(flat, k * EDGE + 128, EDGE, per, second * width + k + 2, 1, float(second), c, False)
    for ref, near, far in ((z_low, 1, 0), (z_high, cols + 2, cols + 3)):
        r = 2.0 + sub(rows)
        geometry(ref, 0, EDGE, rows, 2 * width + near, width, r, float(near), True)
        geometry(ref, 128, EDGE, rows, 2 * width + far, width, r, float(far), False)
        apart = (rows + 1) * width
        r = 1.0 + (rows + 1.0) * sub(2)
        geometry(ref, z_rows, CORNER, 2, width + near, apart, r, float(near), True)
        geometry(ref, z_rows + 136, CORNER, 2, width + far, apart, r, float(far), False)
        apart = (rows + 3) * width
        r = (rows + 3.0) * sub(2)
        geometry(ref, z_rows + 128, CORNER, 2, near, apart, r, float(near), False)
        geometry(ref, z_rows + 144, CORNER, 2, far, apart, r, float(far), False)

    quarter = lax.broadcasted_iota(I32, (128, 128), 1) // ROWS_K
    only = [jnp.where(quarter == k, 1.0, 0.0).astype(BF16) for k in range(4)]

    def block32(ref, index):
        return ref[pl.ds(pl.multiple_of(index * ROWS_K, ROWS_K), ROWS_K), :]

    def turn(indices):
        t = jnp.transpose(jnp.concatenate([block32(row_t, index) for index in indices], axis=0)).astype(BF16)
        for k, index in enumerate(indices):
            side_t[index] = t * only[k]
            side_s[index] = block32(row_s, index).astype(BF16)

    def turn_own(i):
        for k in range(cols // 4):
            index = (i + 2) * width + 2 + 4 * k
            turn([index, index + 1, index + 2, index + 3])

    loop(rows, turn_own)

    def turn_ring(i):
        for r in (i, i + rows + 2):
            for k in range(width // 4):
                index = r * width + 4 * k
                turn([index, index + 1, index + 2, index + 3])
        for r in (2 * i + 2, 2 * i + 3):
            turn([r * width, r * width + 1, r * width + cols + 2, r * width + cols + 3])

    loop(2, turn_ring)

    def density(center, partners, n):
        rhs = jnp.concatenate([side_s[center]] * 4, axis=0)
        total = jnp.zeros((8, 128), F32)
        for j, partner in enumerate(partners):
            y = jnp.maximum(jnp.dot(side_t[partner], rhs, preferred_element_type=F32), 0.0)
            square = y * y
            total = total + jnp.sum((square * y).reshape(16, 8, 128), axis=0)
            if n is not None:
                squares[n, j * 128 : (j + 1) * 128, :] = square.astype(BF16)
        rho[pl.ds(center, 1), :] = jnp.sum(total, axis=0, keepdims=True)

    rho[...] = jnp.ones_like(rho)

    def own_density(i):
        for k in range(16):
            n = i * 16 + k
            r, c = n // cols, n % cols
            center = (r + 2) * width + c + 2
            density(center, [linked(center, codes[j, r, c], width) for j in range(6)], n)

    loop(own // 16, own_density)
    for copy in code_copies:
        copy.wait()

    def ring_cell(center, n):
        density(center, [linked(center, ring_codes[n, j].astype(I32), width) for j in range(6)], None)

    def ring_rows(i):
        for k in range(8):
            c = i * 8 + k
            ring_cell(width + c + 2, c)
            ring_cell((rows + 2) * width + c + 2, cols + c)

    loop(cols // 8, ring_rows)
    for k, r in enumerate([r + 2 for r in range(rows)] + [1, rows + 2]):
        ring_cell(r * width + 1, 2 * cols + k)
        ring_cell(r * width + cols + 2, 2 * cols + rows + 2 + k)

    living = mass[...] > 0.0
    guarded = jnp.where(living, rho[...], 1.0)
    ratio[...] = jnp.where(living, (guarded - 1.0) / (guarded * guarded), 0.0)
    inverse[...] = jnp.where(living, 1.0 / guarded, 0.0)

    def row8(ref, index):
        return rows_of(ref[pl.ds(index, 1), :], 8)

    def shifted(g, r, c):
        off_r = r.astype(F32) - row_mid
        off_c = c.astype(F32) - col_mid
        return jnp.where(sub8 == 0, g + off_r, jnp.where(sub8 == 1, g + off_c, g))

    def positions(g, r, c):
        x = shifted(g, r, c)
        return jnp.where((sub8 == 0) | (sub8 == 4), 1.0, jnp.where(sub8 < 4, pltpu.roll(x, 1, 0), pltpu.roll(x, 5, 0)))

    def features(load, r, c):
        index = r * width + c
        cube = row8(root, index)
        scale = cube * row8(inverse, index)

        g = load(0)
        nu = rows_of(g[7:8], 8)
        first = jnp.where(sub8 < 3, pltpu.roll(g, 5, 0) * nu, jnp.where(sub8 == 6, 1.0, g)) * scale
        press = positions(g, r, c) * jnp.where(sub8 < 4, cube, cube * row8(ratio, index))
        hi, lo = halves(press)
        feat[index, 128:144, :] = jnp.concatenate([hi.astype(F32), lo.astype(F32)], axis=0).astype(BF16)
        feat[index, 0:16, :] = jnp.concatenate([first, load(1) * scale], axis=0).astype(BF16)
        for k in range(1, 8):
            feat[index, 16 * k : 16 * k + 16, :] = jnp.concatenate([load(2 * k) * scale, load(2 * k + 1) * scale], axis=0).astype(BF16)

    def in_cell(ref, n):
        return lambda k: ref[n, 8 * k : 8 * k + 8, :]

    def in_rows(ref, row):
        return lambda k: ref[row + 8 * k : row + 8 * k + 8, :]

    def local_feat(i):
        cells_piece(i).wait()
        for k in range(8):
            n = i * 8 + k
            features(in_cell(cells, n), n // cols + 2, n % cols + 2)

    loop(own // 8, local_feat)

    def a_feat(i):
        for k in range(4):
            n = i * 4 + k
            features(in_cell(a_low, n), jnp.int32(1), n + 2)
            features(in_cell(a_high, n), jnp.int32(rows + 2), n + 2)

    loop(cols // 4, a_feat)
    for ref, c in ((z_low, 1), (z_high, cols + 2)):
        for r in range(rows):
            features(in_rows(ref, r * EDGE), jnp.int32(r + 2), jnp.int32(c))
        for n, r in enumerate((1, rows + 2)):
            features(in_rows(ref, z_rows + n * CORNER), jnp.int32(r), jnp.int32(c))

    def force(n):
        r, c = n // cols, n % cols
        index = (r + 2) * width + c + 2
        lhs = jnp.concatenate([feat[linked(index, codes[j, r, c], width)] for j in range(6)], axis=1)
        sums = jnp.dot(lhs, squares[n], preferred_element_type=F32)
        if masked:
            held = lax.broadcasted_iota(I32, (8, 128), 1) < counts[r, c]

        def load(k):
            value = cells[n, 8 * k : 8 * k + 8, :]
            return jnp.where(held, value, 0.0) if masked else value

        g = load(0)
        m, nu = rows_of(g[6:7], 8), rows_of(g[7:8], 8)
        alive = jnp.where(m > 0.0, time_step, 0.0)
        first = sums[0:8]
        press = sums[128:136] + sums[136:144]
        press = press - positions(g, r + 2, c + 2) * jnp.where(sub8 < 4, rows_of(press[0:1], 8), rows_of(press[4:5], 8))
        press = press * jnp.where(sub8 < 4, row8(ratio, index), 1.0)
        press = press + pltpu.roll(press, 4, 0)
        weight, friction = rows_of(first[6:7], 8), rows_of(first[7:8], 8)
        touching = contact[r, c]
        device, place = touching // per_device, (touching % per_device) * 3
        surface = jnp.where(sub8 == 3, segments[device, place], jnp.where(sub8 == 4, segments[device, place + 1], segments[device, place + 2]))
        wall = wall_gain * jnp.maximum(1.0 - 3.0 * rows_of(g[2:3], 8), 0.0)
        accel = nu * (first - g * weight) + pltpu.roll(first, 3, 0) - g * friction + wall * (surface - g)
        accel = accel - 6.0 * pltpu.roll(press, 2, 0)
        velocity = g + accel * alive
        position = g + time_step * pltpu.roll(velocity, 5, 0)
        out[n, 0:8, :] = jnp.where(sub8 < 3, position, jnp.where(sub8 < 6, velocity, g))
        gain = 2.0 * alive
        stay = 1.0 - gain * weight
        for k in range(1, 16):
            out[n, 8 * k : 8 * k + 8, :] = load(k) * stay + gain * sums[8 * k : 8 * k + 8]
        if not leaving:
            dens[pl.ds(n, 1), :] = jnp.where(m > 0.0, row8(rho, index), 0.0)[0:1]

    def forces(i):
        for k in range(8):
            force(i * 8 + k)
        if not leaving:
            out_piece(i).start()

    loop(own // 8, forces)
    if leaving:
        take_out(out, slots, buffer_row, sent, gathered, out_piece)
    for i in range(own // 8):
        out_piece(i).wait()


def take_out(state, slots, buffer_row, sent, gathered, out_piece):
    leaving, places = slots.shape[0], sent.shape[0]
    offset = jnp.broadcast_to(slots[...], (leaving, 128)) - lax.broadcasted_iota(I32, (leaving, 128), 1)
    gathered[...] = jnp.zeros_like(gathered)
    per = 8

    def body(i):
        hits, parts = [], []
        for k in range(per):
            c = i * per + k
            hit = jnp.where(offset == c * 128, 1.0, 0.0)
            gone = jnp.sum(hit, axis=0, keepdims=True)
            whole = state[c]
            hi, lo = halves(whole)
            hits.append(hit.astype(BF16))
            parts.append(jnp.concatenate([hi, lo], axis=0))
            state[c] = whole * (1.0 - gone)
        gathered[...] += lax.dot_general(jnp.concatenate(hits, axis=1), jnp.concatenate(parts, axis=1), (((1,), (1,)), ((), ())), preferred_element_type=F32)
        out_piece(i).start()

    loop(state.shape[0] // per, body)
    place = jnp.where(jnp.broadcast_to(buffer_row[...], (places, leaving)) == sub_iota((places, leaving)), 1.0, 0.0).astype(BF16)
    right = jnp.concatenate([gathered[...].astype(BF16), jnp.ones((leaving, 128), BF16)], axis=1)
    sums = jnp.dot(place, right, preferred_element_type=F32)
    lane = lax.broadcasted_iota(I32, (places, 128), 1)
    sent[...] = jnp.where((lane == 6) & (sums[:, 256:384] < 0.5), -1.0, sums[:, 0:128] + sums[:, 128:256])


def smem_spec():
    return pl.BlockSpec(memory_space=pltpu.SMEM)


def vmem_spec():
    return pl.BlockSpec(memory_space=pltpu.VMEM)


def step_call(rows, cols, counts, codes, segments, contact, cells, halo, leave=None):
    own = rows * cols
    patch = (rows + 4) * (cols + 4)
    ring = 2 * cols + 2 * (rows + 2)
    new = jax.ShapeDtypeStruct((own, 128, 128), F32)
    extra, first = [], []
    if leave:
        slots, buffer_row, places = leave
        outs = (new, jax.ShapeDtypeStruct((places, 128), F32))
        extra, first = [slots, buffer_row], [pltpu.VMEM((slots.shape[0], 256), F32)]
    else:
        outs = (new, jax.ShapeDtypeStruct((own, 128), F32))
    scalars = [] if counts is None else [counts]
    return pl.pallas_call(
        functools.partial(step_kernel, rows, cols, counts is not None, bool(leave)),
        out_shape=outs,
        in_specs=[smem_spec()] * (len(scalars) + 3) + [any_spec()] + [vmem_spec()] * (4 + len(extra)),
        out_specs=(any_spec(), vmem_spec()),
        scratch_shapes=first
        + [
            pltpu.VMEM((own, 8, 128), F32),
            pltpu.VMEM((own, 128, 128), F32),
            pltpu.VMEM((own, 128, 128), F32),
            pltpu.VMEM((patch, 128, 128), BF16),
            pltpu.VMEM((patch, 32, 128), BF16),
            pltpu.VMEM((patch, 144, 128), BF16),
            pltpu.VMEM((own, 768, 128), BF16),
            pltpu.VMEM((patch * ROWS_K, 128), F32),
            pltpu.VMEM((patch * ROWS_K, 128), F32),
        ]
        + [pltpu.VMEM((patch, 128), F32)] * 5
        + [
            pltpu.SMEM((ring, 128), F32),
            pltpu.SemaphoreType.DMA(()),
            pltpu.SemaphoreType.DMA((own // 8,)),
            pltpu.SemaphoreType.DMA((own // 8,)),
            pltpu.SemaphoreType.DMA((2 + 2 * (rows + 2),)),
        ],
        compiler_params=pltpu.CompilerParams(vmem_limit_bytes=47 * MIB),
    )(*scalars, codes, segments, contact, cells, *halo, *extra)


def insert_kernel(rows, cols, codes, state_in, incoming, slots, out_ref, *refs):
    strips, (state, out, came, left_for, semaphore) = refs[:6], refs[6:]
    arrive = pieces(state_in, state, came, 8)
    leave = pieces(out, out_ref, left_for, 8)
    for i in range(rows * cols // 8):
        arrive(i).start()
    places = slots.shape[0]
    data = incoming[...]
    absent = jnp.broadcast_to(data[:, 6:7], (places, 128)) < 0.0
    offset = jnp.broadcast_to(slots[...], (places, 128)) - lax.broadcasted_iota(I32, (places, 128), 1)
    offset = jnp.where(absent, -1, offset)
    hi, lo = halves(jnp.transpose(data))
    left = jnp.concatenate([hi, lo, jnp.ones((16, places), BF16)], axis=0)
    per = 8

    def body(i):
        arrive(i).wait()
        for pair in range(per // 2):
            first = i * per + pair * 2
            hits = [jnp.where(offset == (first + k) * 128, 1.0, 0.0).astype(BF16) for k in range(2)]
            sums = jnp.dot(left, jnp.concatenate(hits, axis=1), preferred_element_type=F32)
            for k in range(2):
                part = sums[:, 128 * k : 128 * (k + 1)]
                out[first + k] = state[first + k] * (1.0 - part[256:257]) + (part[0:128] + part[128:256])
        leave(i).start()

    loop(rows * cols // per, body)
    copies = fill_strips(rows, cols, out, strips, semaphore)
    for copy in copies:
        copy.start()
    put_strips(rows, cols, codes, lambda r, c: out[r * cols + c, 0:8, :], strips)
    for copy in copies:
        copy.wait()
    for i in range(rows * cols // per):
        leave(i).wait()


def insert(rows, cols, codes, state, incoming, slots):
    own = rows * cols
    return pl.pallas_call(
        functools.partial(insert_kernel, rows, cols),
        out_shape=(jax.ShapeDtypeStruct(state.shape, F32),) + strip_shapes(rows, cols),
        in_specs=[smem_spec(), any_spec(), vmem_spec(), vmem_spec()],
        out_specs=(any_spec(),) + (vmem_spec(),) * 6,
        scratch_shapes=[pltpu.VMEM((own, 128, 128), F32)] * 2 + [pltpu.SemaphoreType.DMA((own // 8,))] * 2 + [pltpu.SemaphoreType.DMA((6 + 2 * rows,))],
        compiler_params=pltpu.CompilerParams(vmem_limit_bytes=52 * MIB),
    )(codes, state, incoming, slots)


def swap(up, down, axis):
    n = lax.axis_size(axis)
    pairs = [(i, (i + 1) % n) for i in range(n if axis == "az" else n - 1)]
    return lax.ppermute(up, axis, pairs), lax.ppermute(down, axis, [(j, i) for i, j in pairs])


def exchange(strips):
    ends_up, ends_down, a_up, a_down, z_up, z_down = strips
    low, high = swap(ends_up, ends_down, "ax")
    a_low, a_high = swap(a_up, a_down, "ax")

    def beside(strip, n):
        return jnp.concatenate([strip.reshape(-1, 128), low[n], high[n]], axis=0)

    sides = beside(z_up, 1), beside(z_down, 0)
    return (a_low, a_high) + swap(*sides, "az"), sides


def local(particles, counts, pair_codes, contact, twist_state, leaving_slot, leaving_dest, arrival_slot):
    rows, cols, fields, block = particles.shape
    ranks = lax.axis_size("ax") * lax.axis_size("az")
    own = rows * cols
    state = particles.reshape(own, fields, block)
    pair_codes = pair_codes.transpose(2, 0, 1)
    halo, sides = exchange(mask_strips(rows, cols, counts, pair_codes, state))

    segments = twist_state.shape[0]
    twist_state, _ = lax.optimization_barrier((twist_state, sides))
    told = jnp.broadcast_to(twist_state.reshape(1, segments * 3), (ranks, segments * 3))
    told = lax.all_to_all(told, AXES, 0, 0, tiled=True)

    dest = leaving_dest[:, 0]
    leaving = dest.shape[0]
    same = dest[:, None] == dest[None, :]
    earlier = lax.broadcasted_iota(I32, (leaving, leaving), 0) > lax.broadcasted_iota(I32, (leaving, leaving), 1)
    order = jnp.sum((same & earlier).astype(I32), axis=1)
    capacity = arrival_slot.shape[0] // ranks
    buffer_row = (dest * capacity + order).reshape(1, leaving)

    leave = (leaving_slot.reshape(-1, 1), buffer_row, ranks * capacity)
    state, outgoing = step_call(rows, cols, counts, pair_codes, told, contact, state, halo, leave)
    incoming = lax.all_to_all(outgoing.reshape(ranks, capacity, fields), AXES, 0, 0, tiled=True)
    state, *strips = insert(rows, cols, pair_codes, state, incoming.reshape(-1, fields), arrival_slot.reshape(-1, 1))
    state, density = step_call(rows, cols, None, pair_codes, told, contact, state, exchange(strips)[0])
    return state.reshape(particles.shape), density.reshape(rows, cols, block)


def solution(mesh):
    both = P("ax", "az")
    flat = P(AXES)
    return jax.shard_map(
        local,
        mesh=mesh,
        in_specs=(P("ax", "az", None, None), both, P("ax", "az", None), both, P(AXES, None), flat, P(AXES, None), flat),
        out_specs=(P("ax", "az", None, None), P("ax", "az", None)),
        check_vma=False,
    )
```

```python
import functools

import jax
import jax.numpy as jnp
from jax import lax
from jax.experimental import pallas as pl
from jax.experimental.pallas import tpu as pltpu
from jax.sharding import PartitionSpec as P

AXES = ("ax", "az")
F32, BF16, I32 = jnp.float32, jnp.bfloat16, jnp.int32

wall_gain = 4.0
time_step = 0.05
MIB = 1 << 20


def rows_of(x, n):
    return jnp.broadcast_to(x, (n,) + x.shape[1:])


def sub_iota(shape):
    return lax.broadcasted_iota(I32, shape, 0)


def halves(x):
    hi = x.astype(BF16)
    return hi, (x - hi.astype(F32)).astype(BF16)


def thirds(x):
    hi = x.astype(BF16).astype(F32)
    rest = x - hi
    mid = rest.astype(BF16).astype(F32)
    return hi, mid, rest - mid


def loop(n, body):
    def step(i, carry):
        body(i)
        return carry

    lax.fori_loop(0, n, step, 0)


ROWS_K = 32
EDGE, CORNER = 136, 152


def live_rows(g, count):
    dead = (sub_iota((8, 128)) == 6) & (lax.broadcasted_iota(I32, (8, 128), 1) >= count)
    return jnp.where(dead, 0.0, g)


def with_codes(behind, codes, r, c):
    lane = lax.broadcasted_iota(I32, (8, 128), 1)
    listed = jnp.zeros((8, 128), F32)
    for j in range(6):
        listed = jnp.where(lane == j, codes[j, r, c].astype(F32), listed)
    return jnp.where(sub_iota((8, 128)) == 7, listed, behind)


def pieces(source, target, semaphore, per):
    def piece(i):
        part = pl.ds(i * per, per)
        return pltpu.make_async_copy(source.at[part], target.at[part], semaphore.at[i])

    return piece


def smem_spec():
    return pl.BlockSpec(memory_space=pltpu.SMEM)


def vmem_spec():
    return pl.BlockSpec(memory_space=pltpu.VMEM)


def any_spec():
    return pl.BlockSpec(memory_space=pl.ANY)


FULL = pltpu.CompilerParams(vmem_limit_bytes=60 * MIB)


def strip_shapes(rows, cols):
    entries = ((2, CORNER), (2, CORNER), (cols, EDGE), (cols, EDGE), (rows, EDGE), (rows, EDGE))
    return tuple(jax.ShapeDtypeStruct((n, height, 128), F32) for n, height in entries)


def put_strips(rows, cols, codes, geo, strips):
    ends_up, ends_down, a_up, a_down, z_up, z_down = strips
    sides = ((ends_up, a_up, rows - 1, rows - 2), (ends_down, a_down, 0, 1))

    def along(i):
        for k in range(4):
            n = i * 4 + k
            for _, strip, first, second in sides:
                strip[n, 0:8, :] = geo(first, n)
                strip[n, 128:136, :] = with_codes(geo(second, n), codes, first, n)

    loop(cols // 4, along)
    for strip, first, second in ((z_up, cols - 1, cols - 2), (z_down, 0, 1)):
        for r in range(rows):
            strip[r, 0:8, :] = geo(r, first)
            strip[r, 128:136, :] = with_codes(geo(r, second), codes, r, first)
    for strip, _, first, second in sides:
        for n, (near, far) in enumerate(((0, 1), (cols - 1, cols - 2))):
            strip[n, 0:8, :] = geo(first, near)
            strip[n, 128:136, :] = with_codes(geo(second, near), codes, first, near)
            strip[n, 136:144, :] = geo(first, far)
            strip[n, 144:152, :] = geo(second, far)


def fill_strips(rows, cols, state, strips, semaphore):
    ends_up, ends_down, a_up, a_down, z_up, z_down = strips
    parts = []
    for ends, strip, r in ((ends_up, a_up, rows - 1), (ends_down, a_down, 0)):
        parts.append((state.at[pl.ds(r * cols, cols), 8:128, :], strip.at[:, 8:128, :]))
        for n, c in enumerate((0, cols - 1)):
            parts.append((state.at[r * cols + c, 8:128, :], ends.at[n, 8:128, :]))
    for strip, c in ((z_up, cols - 1), (z_down, 0)):
        for r in range(rows):
            parts.append((state.at[r * cols + c, 8:128, :], strip.at[r, 8:128, :]))
    return [pltpu.make_async_copy(a, b, semaphore.at[k]) for k, (a, b) in enumerate(parts)]


def mask_kernel(rows, cols, counts, codes, state, *refs):
    strips, (rows8, came, semaphore) = refs[:6], refs[6:]
    first = pltpu.make_async_copy(state.at[:, 0:8, :], rows8, came)
    first.start()
    copies = fill_strips(rows, cols, state, strips, semaphore)
    for copy in copies:
        copy.start()
    first.wait()
    put_strips(rows, cols, codes, lambda r, c: live_rows(rows8[r * cols + c], counts[r, c]), strips)
    for copy in copies:
        copy.wait()


def mask_strips(rows, cols, counts, codes, state):
    return pl.pallas_call(
        functools.partial(mask_kernel, rows, cols),
        out_shape=strip_shapes(rows, cols),
        in_specs=[smem_spec(), smem_spec(), any_spec()],
        out_specs=(vmem_spec(),) * 6,
        scratch_shapes=[pltpu.VMEM((rows * cols, 8, 128), F32), pltpu.SemaphoreType.DMA(()), pltpu.SemaphoreType.DMA((6 + 2 * rows,))],
        compiler_params=FULL,
    )(counts, codes, state)


def linked(center, code, width):
    up = (code * 11) >> 5
    return center + up * (width - 3) + code - (width + 1)


def makers(rows, cols, row_t, row_s, side_t, side_s, mass, root, rho, squares):
    width = cols + 4
    row_mid, col_mid = (rows + 3) / 2.0, (cols + 3) / 2.0

    def geometry(flat, row, stride, n, index, apart, r, c, center, limit=None):
        def field(k):
            return flat[pl.ds(row + k, n, stride=stride), :]

        x = [field(0) + (r - row_mid), field(1) + (c - col_mid), field(2)]
        norm = x[0] * x[0] + x[1] * x[1] + x[2] * x[2]
        m = field(6)
        if limit is not None:
            m = jnp.where(lax.broadcasted_iota(I32, (n, 128), 1) < limit, m, 0.0)
        cube = jnp.exp2(jnp.log2(jnp.maximum(m, 1e-30)) * (1.0 / 3.0))
        cube = cube - (cube - m / (cube * cube)) * (1.0 / 3.0)
        cube = jnp.where(m > 0.0, cube, 0.0)

        def put(target, k, value):
            target[pl.ds(index * ROWS_K + k, n, stride=apart * ROWS_K), :] = value

        for k, value in enumerate([x[0] * cube, x[1] * cube, x[2] * cube, -norm * cube, cube]):
            hi, mid, low = thirds(value)
            for block, piece in enumerate((hi, mid, low, hi, mid, hi)):
                put(row_t, 5 * block + k, piece)
        put(row_t, 30, jnp.zeros_like(m))
        put(row_t, 31, jnp.zeros_like(m))
        for k in range(n):
            mass[pl.ds(index + k * apart, 1), :] = m[k : k + 1]
            root[pl.ds(index + k * apart, 1), :] = cube[k : k + 1]
        if center:
            for k, value in enumerate([x[0] + x[0], x[1] + x[1], x[2] + x[2], jnp.ones_like(m), 1.0 - norm]):
                hi, mid, low = thirds(value)
                for block, piece in enumerate((hi, hi, hi, mid, mid, low)):
                    put(row_s, 5 * block + k, piece)
            put(row_s, 30, jnp.zeros_like(m))
            put(row_s, 31, jnp.zeros_like(m))

    def sub(n):
        return sub_iota((n, 128)).astype(F32)

    quarter = lax.broadcasted_iota(I32, (128, 128), 1) // ROWS_K
    only = [jnp.where(quarter == k, 1.0, 0.0).astype(BF16) for k in range(4)]

    def block32(ref, index):
        return ref[pl.ds(pl.multiple_of(index * ROWS_K, ROWS_K), ROWS_K), :]

    def turn(indices):
        t = jnp.transpose(jnp.concatenate([block32(row_t, index) for index in indices], axis=0)).astype(BF16)
        for k, index in enumerate(indices):
            side_t[index] = t * only[k]
            side_s[index] = block32(row_s, index).astype(BF16)

    def density(center, partners, n):
        rhs = jnp.concatenate([side_s[center]] * 4, axis=0)
        total = jnp.zeros((8, 128), F32)
        for j, partner in enumerate(partners):
            y = jnp.maximum(jnp.dot(side_t[partner], rhs, preferred_element_type=F32), 0.0)
            square = y * y
            total = total + jnp.sum((square * y).reshape(16, 8, 128), axis=0)
            if n is not None:
                squares[n, j * 128 : (j + 1) * 128, :] = square.astype(BF16)
        rho[pl.ds(center, 1), :] = jnp.sum(total, axis=0, keepdims=True)

    return geometry, sub, turn, density


def own_copies(rows, cols, pairs, semaphore):
    width = cols + 4
    copies = []
    for source, target in pairs:
        for r in range(rows):
            part = pl.ds((r + 2) * width + 2, cols)
            copies.append(pltpu.make_async_copy(source.at[part], target.at[part], semaphore.at[len(copies)]))
    return copies


def inner_copies(rows, cols, source, target, semaphore):
    parts = [pl.ds(r * cols + 1, cols - 2) for r in range(1, rows - 1)]
    return [pltpu.make_async_copy(source.at[part], target.at[part], semaphore.at[k]) for k, part in enumerate(parts)]


def own_kernel(rows, cols, masked, *refs):
    if masked:
        counts, refs = refs[0], refs[1:]
    codes, cells_in, side_t_out, side_s_out, squares_out, mass, root, rho = refs[:8]
    geo, side_t, side_s, squares, row_t, row_s, geo_came, sides_left, squares_left = refs[8:]
    width = cols + 4
    own = rows * cols
    per = 8
    geometry, sub, turn, density = makers(rows, cols, row_t, row_s, side_t, side_s, mass, root, rho, squares)
    geo_copy = pltpu.make_async_copy(cells_in.at[:, 0:8, :], geo, geo_came)
    geo_copy.start()
    for ref in (mass, root, rho):
        ref[...] = jnp.ones_like(ref)
    geo_copy.wait()
    geo_flat = geo.reshape(own * 8, 128)

    def local_geo(i):
        first = i * per
        r, c = first // cols + 2, first % cols + 2
        limit = None
        if masked:
            limit = jnp.zeros((per, 128), I32)
            for k in range(per):
                limit = jnp.where(sub_iota((per, 128)) == k, counts[first // cols, first % cols + k], limit)
        geometry(geo_flat, first * 8, 8, per, r * width + c, 1, r.astype(F32), c.astype(F32) + sub(per), True, limit)

    loop(own // per, local_geo)
    def turn_own(i):
        for k in range(cols // 4):
            index = (i + 2) * width + 2 + 4 * k
            turn([index, index + 1, index + 2, index + 3])

    loop(rows, turn_own)

    sides = own_copies(rows, cols, ((side_t, side_t_out), (side_s, side_s_out)), sides_left)
    for copy in sides:
        copy.start()

    def inner_density(i):
        r = i + 1
        for k in range(1, cols - 1):
            center = (r + 2) * width + k + 2
            density(center, [linked(center, codes[j, r, k], width) for j in range(6)], r * cols + k)

    loop(rows - 2, inner_density)
    inner = inner_copies(rows, cols, squares, squares_out, squares_left)
    for copy in inner:
        copy.start()
    for copy in sides + inner:
        copy.wait()


def own_call(rows, cols, counts, codes, cells):
    own = rows * cols
    patch = (rows + 4) * (cols + 4)
    scalars = [] if counts is None else [counts]
    field = jax.ShapeDtypeStruct((patch, 128), F32)
    return pl.pallas_call(
        functools.partial(own_kernel, rows, cols, counts is not None),
        out_shape=(jax.ShapeDtypeStruct((patch, 128, 128), BF16), jax.ShapeDtypeStruct((patch, 32, 128), BF16), jax.ShapeDtypeStruct((own, 768, 128), BF16), field, field, field),
        in_specs=[smem_spec()] * (len(scalars) + 1) + [any_spec()],
        out_specs=(any_spec(),) * 3 + (vmem_spec(),) * 3,
        scratch_shapes=[
            pltpu.VMEM((own, 8, 128), F32),
            pltpu.VMEM((patch, 128, 128), BF16),
            pltpu.VMEM((patch, 32, 128), BF16),
            pltpu.VMEM((own, 768, 128), BF16),
            pltpu.VMEM((patch * ROWS_K, 128), F32),
            pltpu.VMEM((patch * ROWS_K, 128), F32),
            pltpu.SemaphoreType.DMA(()),
            pltpu.SemaphoreType.DMA((2 * rows,)),
            pltpu.SemaphoreType.DMA((rows - 2,)),
        ],
        compiler_params=pltpu.CompilerParams(vmem_limit_bytes=47 * MIB),
        cost_estimate=pl.CostEstimate(flops=5 * 10**9, bytes_accessed=16 * MIB, transcendentals=0),
    )(*scalars, codes, cells)


def step_kernel(rows, cols, masked, leaving, ahead, *refs):
    if masked:
        counts, refs = refs[0], refs[1:]
    codes, segments, contact, cells_in, a_low, a_high, z_low, z_high = refs[:8]
    if ahead:
        side_t_in, side_s_in, squares_in, mass_in, root_in, rho_in = refs[8:14]
        refs = refs[:8] + refs[14:]
    if leaving:
        slots, buffer_row, out_ref, sent, gathered = refs[8:13]
        refs = refs[13:]
    else:
        out_ref, dens = refs[8:10]
        refs = refs[10:]
    geo, cells, out, side_t, side_s, feat, squares, row_t, row_s = refs[:9]
    mass, root, rho, ratio, inverse, ring_codes, geo_came, sides_came, squares_came, cells_came, out_left, codes_came = refs[9:]
    width = cols + 4
    own = rows * cols
    z_rows = rows * EDGE
    per_device = segments.shape[1] // 3
    sub8 = sub_iota((8, 128))
    row_mid, col_mid = (rows + 3) / 2.0, (cols + 3) / 2.0

    if not ahead:
        geo_copy = pltpu.make_async_copy(cells_in.at[:, 0:8, :], geo, geo_came)
        geo_copy.start()
    code_copies = []

    def bring_codes(source, first, n):
        code_copies.append(pltpu.make_async_copy(source, ring_codes.at[pl.ds(first, n), :], codes_came.at[len(code_copies)]))

    bring_codes(a_low.at[:, EDGE - 1, :], 0, cols)
    bring_codes(a_high.at[:, EDGE - 1, :], cols, cols)
    for ref, first in ((z_low, 2 * cols), (z_high, 2 * cols + rows + 2)):
        for r in range(rows):
            bring_codes(ref.at[pl.ds(r * EDGE + EDGE - 1, 1), :], first + r, 1)
        for n in range(2):
            bring_codes(ref.at[pl.ds(z_rows + n * CORNER + EDGE - 1, 1), :], first + rows + n, 1)
    cells_piece = pieces(cells_in, cells, cells_came, 8)
    out_piece = pieces(out, out_ref, out_left, 8)
    for copy in code_copies:
        copy.start()
    for i in range(own // 8):
        cells_piece(i).start()

    geometry, sub, turn, density = makers(rows, cols, row_t, row_s, side_t, side_s, mass, root, rho, squares)
    per = 8
    if ahead:
        for copy in own_copies(rows, cols, ((side_t_in, side_t), (side_s_in, side_s)), sides_came) + inner_copies(rows, cols, squares_in, squares, squares_came):
            copy.start()
        for source, target in ((mass_in, mass), (root_in, root), (rho_in, rho)):
            target[...] = source[...]
    else:
        rho[...] = jnp.ones_like(rho)
        geo_copy.wait()
    geo_flat = geo.reshape(own * 8, 128)

    def local_geo(i):
        first = i * per
        r, c = first // cols + 2, first % cols + 2
        limit = None
        if masked:
            limit = jnp.zeros((per, 128), I32)
            for k in range(per):
                limit = jnp.where(sub_iota((per, 128)) == k, counts[first // cols, first % cols + k], limit)
        geometry(geo_flat, first * 8, 8, per, r * width + c, 1, r.astype(F32), c.astype(F32) + sub(per), True, limit)

    if not ahead:
        loop(own // per, local_geo)
    for ref, first, second in ((a_low, 1, 0), (a_high, rows + 2, rows + 3)):
        flat = ref.reshape(cols * EDGE, 128)
        for k in range(0, cols, per):
            c = k + 2.0 + sub(per)
            geometry(flat, k * EDGE, EDGE, per, first * width + k + 2, 1, float(first), c, True)
            geometry(flat, k * EDGE + 128, EDGE, per, second * width + k + 2, 1, float(second), c, False)
    for ref, near, far in ((z_low, 1, 0), (z_high, cols + 2, cols + 3)):
        r = 2.0 + sub(rows)
        geometry(ref, 0, EDGE, rows, 2 * width + near, width, r, float(near), True)
        geometry(ref, 128, EDGE, rows, 2 * width + far, width, r, float(far), False)
        apart = (rows + 1) * width
        r = 1.0 + (rows + 1.0) * sub(2)
        geometry(ref, z_rows, CORNER, 2, width + near, apart, r, float(near), True)
        geometry(ref, z_rows + 136, CORNER, 2, width + far, apart, r, float(far), False)
        apart = (rows + 3) * width
        r = (rows + 3.0) * sub(2)
        geometry(ref, z_rows + 128, CORNER, 2, near, apart, r, float(near), False)
        geometry(ref, z_rows + 144, CORNER, 2, far, apart, r, float(far), False)

    def turn_own(i):
        for k in range(cols // 4):
            index = (i + 2) * width + 2 + 4 * k
            turn([index, index + 1, index + 2, index + 3])

    if not ahead:
        loop(rows, turn_own)

    def turn_ring(i):
        for r in (i, i + rows + 2):
            for k in range(width // 4):
                index = r * width + 4 * k
                turn([index, index + 1, index + 2, index + 3])
        for r in (2 * i + 2, 2 * i + 3):
            turn([r * width, r * width + 1, r * width + cols + 2, r * width + cols + 3])

    loop(2, turn_ring)

    def own_cell(r, c):
        center = (r + 2) * width + c + 2
        density(center, [linked(center, codes[j, r, c], width) for j in range(6)], r * cols + c)

    def whole_row(r):
        for c in range(cols):
            own_cell(r, c)

    if ahead:
        for copy in own_copies(rows, cols, ((side_t_in, side_t), (side_s_in, side_s)), sides_came):
            copy.wait()
        loop(2, lambda i: whole_row(i * (rows - 1)))
        for r in range(1, rows - 1):
            own_cell(r, 0)
            own_cell(r, cols - 1)
    else:
        loop(rows, whole_row)
    for copy in code_copies:
        copy.wait()

    def ring_cell(center, n):
        density(center, [linked(center, ring_codes[n, j].astype(I32), width) for j in range(6)], None)

    def ring_rows(i):
        for k in range(8):
            c = i * 8 + k
            ring_cell(width + c + 2, c)
            ring_cell((rows + 2) * width + c + 2, cols + c)

    loop(cols // 8, ring_rows)
    for k, r in enumerate([r + 2 for r in range(rows)] + [1, rows + 2]):
        ring_cell(r * width + 1, 2 * cols + k)
        ring_cell(r * width + cols + 2, 2 * cols + rows + 2 + k)

    living = mass[...] > 0.0
    guarded = jnp.where(living, rho[...], 1.0)
    ratio[...] = jnp.where(living, (guarded - 1.0) / (guarded * guarded), 0.0)
    inverse[...] = jnp.where(living, 1.0 / guarded, 0.0)

    def row8(ref, index):
        return rows_of(ref[pl.ds(index, 1), :], 8)

    def shifted(g, r, c):
        off_r = r.astype(F32) - row_mid
        off_c = c.astype(F32) - col_mid
        return jnp.where(sub8 == 0, g + off_r, jnp.where(sub8 == 1, g + off_c, g))

    def positions(g, r, c):
        x = shifted(g, r, c)
        return jnp.where((sub8 == 0) | (sub8 == 4), 1.0, jnp.where(sub8 < 4, pltpu.roll(x, 1, 0), pltpu.roll(x, 5, 0)))

    def features(load, r, c):
        index = r * width + c
        cube = row8(root, index)
        scale = cube * row8(inverse, index)

        g = load(0)
        nu = rows_of(g[7:8], 8)
        first = jnp.where(sub8 < 3, pltpu.roll(g, 5, 0) * nu, jnp.where(sub8 == 6, 1.0, g)) * scale
        press = positions(g, r, c) * jnp.where(sub8 < 4, cube, cube * row8(ratio, index))
        hi, lo = halves(press)
        feat[index, 128:144, :] = jnp.concatenate([hi.astype(F32), lo.astype(F32)], axis=0).astype(BF16)
        feat[index, 0:16, :] = jnp.concatenate([first, load(1) * scale], axis=0).astype(BF16)
        for k in range(1, 8):
            feat[index, 16 * k : 16 * k + 16, :] = jnp.concatenate([load(2 * k) * scale, load(2 * k + 1) * scale], axis=0).astype(BF16)

    def in_cell(ref, n):
        return lambda k: ref[n, 8 * k : 8 * k + 8, :]

    def in_rows(ref, row):
        return lambda k: ref[row + 8 * k : row + 8 * k + 8, :]

    def local_feat(i):
        cells_piece(i).wait()
        for k in range(8):
            n = i * 8 + k
            features(in_cell(cells, n), n // cols + 2, n % cols + 2)

    if ahead:
        for copy in inner_copies(rows, cols, squares_in, squares, squares_came):
            copy.wait()
    loop(own // 8, local_feat)

    def a_feat(i):
        for k in range(4):
            n = i * 4 + k
            features(in_cell(a_low, n), jnp.int32(1), n + 2)
            features(in_cell(a_high, n), jnp.int32(rows + 2), n + 2)

    loop(cols // 4, a_feat)
    for ref, c in ((z_low, 1), (z_high, cols + 2)):
        for r in range(rows):
            features(in_rows(ref, r * EDGE), jnp.int32(r + 2), jnp.int32(c))
        for n, r in enumerate((1, rows + 2)):
            features(in_rows(ref, z_rows + n * CORNER), jnp.int32(r), jnp.int32(c))

    def force(n):
        r, c = n // cols, n % cols
        index = (r + 2) * width + c + 2
        lhs = jnp.concatenate([feat[linked(index, codes[j, r, c], width)] for j in range(6)], axis=1)
        sums = jnp.dot(lhs, squares[n], preferred_element_type=F32)
        if masked:
            held = lax.broadcasted_iota(I32, (8, 128), 1) < counts[r, c]

        def load(k):
            value = cells[n, 8 * k : 8 * k + 8, :]
            return jnp.where(held, value, 0.0) if masked else value

        g = load(0)
        m, nu = rows_of(g[6:7], 8), rows_of(g[7:8], 8)
        alive = jnp.where(m > 0.0, time_step, 0.0)
        first = sums[0:8]
        press = sums[128:136] + sums[136:144]
        press = press - positions(g, r + 2, c + 2) * jnp.where(sub8 < 4, rows_of(press[0:1], 8), rows_of(press[4:5], 8))
        press = press * jnp.where(sub8 < 4, row8(ratio, index), 1.0)
        press = press + pltpu.roll(press, 4, 0)
        weight, friction = rows_of(first[6:7], 8), rows_of(first[7:8], 8)
        touching = contact[r, c]
        device, place = touching // per_device, (touching % per_device) * 3
        surface = jnp.where(sub8 == 3, segments[device, place], jnp.where(sub8 == 4, segments[device, place + 1], segments[device, place + 2]))
        wall = wall_gain * jnp.maximum(1.0 - 3.0 * rows_of(g[2:3], 8), 0.0)
        accel = nu * (first - g * weight) + pltpu.roll(first, 3, 0) - g * friction + wall * (surface - g)
        accel = accel - 6.0 * pltpu.roll(press, 2, 0)
        velocity = g + accel * alive
        position = g + time_step * pltpu.roll(velocity, 5, 0)
        out[n, 0:8, :] = jnp.where(sub8 < 3, position, jnp.where(sub8 < 6, velocity, g))
        gain = 2.0 * alive
        stay = 1.0 - gain * weight
        for k in range(1, 16):
            out[n, 8 * k : 8 * k + 8, :] = load(k) * stay + gain * sums[8 * k : 8 * k + 8]
        if not leaving:
            dens[pl.ds(n, 1), :] = jnp.where(m > 0.0, row8(rho, index), 0.0)[0:1]

    def forces(i):
        for k in range(8):
            force(i * 8 + k)
        if not leaving:
            out_piece(i).start()

    loop(own // 8, forces)
    if leaving:
        take_out(out, slots, buffer_row, sent, gathered, out_piece)
    for i in range(own // 8):
        out_piece(i).wait()


def take_out(state, slots, buffer_row, sent, gathered, out_piece):
    leaving, places = slots.shape[0], sent.shape[0]
    offset = jnp.broadcast_to(slots[...], (leaving, 128)) - lax.broadcasted_iota(I32, (leaving, 128), 1)
    gathered[...] = jnp.zeros_like(gathered)
    per = 8

    def body(i):
        hits, parts = [], []
        for k in range(per):
            c = i * per + k
            hit = jnp.where(offset == c * 128, 1.0, 0.0)
            gone = jnp.sum(hit, axis=0, keepdims=True)
            whole = state[c]
            hi, lo = halves(whole)
            hits.append(hit.astype(BF16))
            parts.append(jnp.concatenate([hi, lo], axis=0))
            state[c] = whole * (1.0 - gone)
        gathered[...] += lax.dot_general(jnp.concatenate(hits, axis=1), jnp.concatenate(parts, axis=1), (((1,), (1,)), ((), ())), preferred_element_type=F32)
        out_piece(i).start()

    loop(state.shape[0] // per, body)
    place = jnp.where(jnp.broadcast_to(buffer_row[...], (places, leaving)) == sub_iota((places, leaving)), 1.0, 0.0).astype(BF16)
    right = jnp.concatenate([gathered[...].astype(BF16), jnp.ones((leaving, 128), BF16)], axis=1)
    sums = jnp.dot(place, right, preferred_element_type=F32)
    lane = lax.broadcasted_iota(I32, (places, 128), 1)
    sent[...] = jnp.where((lane == 6) & (sums[:, 256:384] < 0.5), -1.0, sums[:, 0:128] + sums[:, 128:256])


def smem_spec():
    return pl.BlockSpec(memory_space=pltpu.SMEM)


def vmem_spec():
    return pl.BlockSpec(memory_space=pltpu.VMEM)


def step_call(rows, cols, counts, codes, segments, contact, cells, halo, ahead, leave=None):
    own = rows * cols
    patch = (rows + 4) * (cols + 4)
    ring = 2 * cols + 2 * (rows + 2)
    new = jax.ShapeDtypeStruct((own, 128, 128), F32)
    extra, first = [], []
    if leave:
        slots, buffer_row, places = leave
        outs = (new, jax.ShapeDtypeStruct((places, 128), F32))
        extra, first = [slots, buffer_row], [pltpu.VMEM((slots.shape[0], 256), F32)]
    else:
        outs = (new, jax.ShapeDtypeStruct((own, 128), F32))
    scalars = [] if counts is None else [counts]
    return pl.pallas_call(
        functools.partial(step_kernel, rows, cols, counts is not None, bool(leave), ahead is not None),
        out_shape=outs,
        in_specs=[smem_spec()] * (len(scalars) + 3) + [any_spec()] + [vmem_spec()] * 4 + ([] if ahead is None else [any_spec()] * 3 + [vmem_spec()] * 3) + [vmem_spec()] * len(extra),
        out_specs=(any_spec(), vmem_spec()),
        scratch_shapes=first
        + [
            pltpu.VMEM((own, 8, 128), F32),
            pltpu.VMEM((own, 128, 128), F32),
            pltpu.VMEM((own, 128, 128), F32),
            pltpu.VMEM((patch, 128, 128), BF16),
            pltpu.VMEM((patch, 32, 128), BF16),
            pltpu.VMEM((patch, 144, 128), BF16),
            pltpu.VMEM((own, 768, 128), BF16),
            pltpu.VMEM((patch * ROWS_K, 128), F32),
            pltpu.VMEM((patch * ROWS_K, 128), F32),
        ]
        + [pltpu.VMEM((patch, 128), F32)] * 5
        + [
            pltpu.SMEM((ring, 128), F32),
            pltpu.SemaphoreType.DMA(()),
            pltpu.SemaphoreType.DMA((2 * rows,)),
            pltpu.SemaphoreType.DMA((rows - 2,)),
            pltpu.SemaphoreType.DMA((own // 8,)),
            pltpu.SemaphoreType.DMA((own // 8,)),
            pltpu.SemaphoreType.DMA((2 + 2 * (rows + 2),)),
        ],
        compiler_params=pltpu.CompilerParams(vmem_limit_bytes=47 * MIB),
    )(*scalars, codes, segments, contact, cells, *halo, *(ahead or ()), *extra)


def insert_kernel(rows, cols, codes, state_in, incoming, slots, out_ref, *refs):
    strips, (state, out, came, left_for, semaphore) = refs[:6], refs[6:]
    arrive = pieces(state_in, state, came, 8)
    leave = pieces(out, out_ref, left_for, 8)
    for i in range(rows * cols // 8):
        arrive(i).start()
    places = slots.shape[0]
    data = incoming[...]
    absent = jnp.broadcast_to(data[:, 6:7], (places, 128)) < 0.0
    offset = jnp.broadcast_to(slots[...], (places, 128)) - lax.broadcasted_iota(I32, (places, 128), 1)
    offset = jnp.where(absent, -1, offset)
    hi, lo = halves(jnp.transpose(data))
    left = jnp.concatenate([hi, lo, jnp.ones((16, places), BF16)], axis=0)
    per = 8

    def body(i):
        arrive(i).wait()
        for pair in range(per // 2):
            first = i * per + pair * 2
            hits = [jnp.where(offset == (first + k) * 128, 1.0, 0.0).astype(BF16) for k in range(2)]
            sums = jnp.dot(left, jnp.concatenate(hits, axis=1), preferred_element_type=F32)
            for k in range(2):
                part = sums[:, 128 * k : 128 * (k + 1)]
                out[first + k] = state[first + k] * (1.0 - part[256:257]) + (part[0:128] + part[128:256])
        leave(i).start()

    loop(rows * cols // per, body)
    copies = fill_strips(rows, cols, out, strips, semaphore)
    for copy in copies:
        copy.start()
    put_strips(rows, cols, codes, lambda r, c: out[r * cols + c, 0:8, :], strips)
    for copy in copies:
        copy.wait()
    for i in range(rows * cols // per):
        leave(i).wait()


def insert(rows, cols, codes, state, incoming, slots):
    own = rows * cols
    return pl.pallas_call(
        functools.partial(insert_kernel, rows, cols),
        out_shape=(jax.ShapeDtypeStruct(state.shape, F32),) + strip_shapes(rows, cols),
        in_specs=[smem_spec(), any_spec(), vmem_spec(), vmem_spec()],
        out_specs=(any_spec(),) + (vmem_spec(),) * 6,
        scratch_shapes=[pltpu.VMEM((own, 128, 128), F32)] * 2 + [pltpu.SemaphoreType.DMA((own // 8,))] * 2 + [pltpu.SemaphoreType.DMA((6 + 2 * rows,))],
        compiler_params=pltpu.CompilerParams(vmem_limit_bytes=52 * MIB),
    )(codes, state, incoming, slots)


def swap(up, down, axis):
    n = lax.axis_size(axis)
    pairs = [(i, (i + 1) % n) for i in range(n if axis == "az" else n - 1)]
    return lax.ppermute(up, axis, pairs), lax.ppermute(down, axis, [(j, i) for i, j in pairs])


def exchange(strips):
    ends_up, ends_down, a_up, a_down, z_up, z_down = strips
    low, high = swap(ends_up, ends_down, "ax")
    a_low, a_high = swap(a_up, a_down, "ax")

    def beside(strip, n):
        return jnp.concatenate([strip.reshape(-1, 128), low[n], high[n]], axis=0)

    sides = beside(z_up, 1), beside(z_down, 0)
    return (a_low, a_high) + swap(*sides, "az"), sides


def local(particles, counts, pair_codes, contact, twist_state, leaving_slot, leaving_dest, arrival_slot):
    rows, cols, fields, block = particles.shape
    ranks = lax.axis_size("ax") * lax.axis_size("az")
    own = rows * cols
    state = particles.reshape(own, fields, block)
    pair_codes = pair_codes.transpose(2, 0, 1)
    halo, sides = exchange(mask_strips(rows, cols, counts, pair_codes, state))

    segments = twist_state.shape[0]
    twist_state, _ = lax.optimization_barrier((twist_state, sides))
    told = jnp.broadcast_to(twist_state.reshape(1, segments * 3), (ranks, segments * 3))
    told = lax.all_to_all(told, AXES, 0, 0, tiled=True)

    dest = leaving_dest[:, 0]
    leaving = dest.shape[0]
    same = dest[:, None] == dest[None, :]
    earlier = lax.broadcasted_iota(I32, (leaving, leaving), 0) > lax.broadcasted_iota(I32, (leaving, leaving), 1)
    order = jnp.sum((same & earlier).astype(I32), axis=1)
    capacity = arrival_slot.shape[0] // ranks
    buffer_row = (dest * capacity + order).reshape(1, leaving)

    leave = (leaving_slot.reshape(-1, 1), buffer_row, ranks * capacity)
    state, outgoing = step_call(rows, cols, counts, pair_codes, told, contact, state, halo, None, leave)
    incoming = lax.all_to_all(outgoing.reshape(ranks, capacity, fields), AXES, 0, 0, tiled=True)
    state, *strips = insert(rows, cols, pair_codes, state, incoming.reshape(-1, fields), arrival_slot.reshape(-1, 1))
    halo, sides = exchange(strips)
    ahead = own_call(rows, cols, None, pair_codes, lax.optimization_barrier((state, sides))[0])
    state, density = step_call(rows, cols, None, pair_codes, told, contact, state, halo, ahead)
    return state.reshape(particles.shape), density.reshape(rows, cols, block)


def solution(mesh):
    both = P("ax", "az")
    flat = P(AXES)
    return jax.shard_map(
        local,
        mesh=mesh,
        in_specs=(P("ax", "az", None, None), both, P("ax", "az", None), both, P(AXES, None), flat, P(AXES, None), flat),
        out_specs=(P("ax", "az", None, None), P("ax", "az", None)),
        check_vma=False,
    )
```

```python
import functools

import jax
import jax.numpy as jnp
from jax import lax
from jax.experimental import pallas as pl
from jax.experimental.pallas import tpu as pltpu
from jax.sharding import PartitionSpec as P

AXES = ("ax", "az")
F32, BF16, I32 = jnp.float32, jnp.bfloat16, jnp.int32

wall_gain = 4.0
time_step = 0.05
MIB = 1 << 20


def rows_of(x, n):
    return jnp.broadcast_to(x, (n,) + x.shape[1:])


def sub_iota(shape):
    return lax.broadcasted_iota(I32, shape, 0)


def halves(x):
    hi = x.astype(BF16)
    return hi, (x - hi.astype(F32)).astype(BF16)


def thirds(x):
    hi = x.astype(BF16).astype(F32)
    rest = x - hi
    mid = rest.astype(BF16).astype(F32)
    return hi, mid, rest - mid


def loop(n, body):
    def step(i, carry):
        body(i)
        return carry

    lax.fori_loop(0, n, step, 0)


ROWS_K = 32
EDGE, CORNER = 136, 152


def live_rows(g, count):
    dead = (sub_iota((8, 128)) == 6) & (lax.broadcasted_iota(I32, (8, 128), 1) >= count)
    return jnp.where(dead, 0.0, g)


def with_codes(behind, codes, r, c):
    lane = lax.broadcasted_iota(I32, (8, 128), 1)
    listed = jnp.zeros((8, 128), F32)
    for j in range(6):
        listed = jnp.where(lane == j, codes[j, r, c].astype(F32), listed)
    return jnp.where(sub_iota((8, 128)) == 7, listed, behind)


def pieces(source, target, semaphore, per):
    def piece(i):
        part = pl.ds(i * per, per)
        return pltpu.make_async_copy(source.at[part], target.at[part], semaphore.at[i])

    return piece


def smem_spec():
    return pl.BlockSpec(memory_space=pltpu.SMEM)


def vmem_spec():
    return pl.BlockSpec(memory_space=pltpu.VMEM)


def any_spec():
    return pl.BlockSpec(memory_space=pl.ANY)


FULL = pltpu.CompilerParams(vmem_limit_bytes=60 * MIB)


def strip_shapes(rows, cols):
    entries = ((2, CORNER), (2, CORNER), (cols, EDGE), (cols, EDGE), (rows, EDGE), (rows, EDGE))
    return tuple(jax.ShapeDtypeStruct((n, height, 128), F32) for n, height in entries)


def put_strips(rows, cols, codes, geo, strips):
    ends_up, ends_down, a_up, a_down, z_up, z_down = strips
    sides = ((ends_up, a_up, rows - 1, rows - 2), (ends_down, a_down, 0, 1))

    def along(i):
        for k in range(4):
            n = i * 4 + k
            for _, strip, first, second in sides:
                strip[n, 0:8, :] = geo(first, n)
                strip[n, 128:136, :] = with_codes(geo(second, n), codes, first, n)

    loop(cols // 4, along)
    for strip, first, second in ((z_up, cols - 1, cols - 2), (z_down, 0, 1)):
        for r in range(rows):
            strip[r, 0:8, :] = geo(r, first)
            strip[r, 128:136, :] = with_codes(geo(r, second), codes, r, first)
    for strip, _, first, second in sides:
        for n, (near, far) in enumerate(((0, 1), (cols - 1, cols - 2))):
            strip[n, 0:8, :] = geo(first, near)
            strip[n, 128:136, :] = with_codes(geo(second, near), codes, first, near)
            strip[n, 136:144, :] = geo(first, far)
            strip[n, 144:152, :] = geo(second, far)


def fill_strips(rows, cols, state, strips, semaphore):
    ends_up, ends_down, a_up, a_down, z_up, z_down = strips
    parts = []
    for ends, strip, r in ((ends_up, a_up, rows - 1), (ends_down, a_down, 0)):
        parts.append((state.at[pl.ds(r * cols, cols), 8:128, :], strip.at[:, 8:128, :]))
        for n, c in enumerate((0, cols - 1)):
            parts.append((state.at[r * cols + c, 8:128, :], ends.at[n, 8:128, :]))
    for strip, c in ((z_up, cols - 1), (z_down, 0)):
        for r in range(rows):
            parts.append((state.at[r * cols + c, 8:128, :], strip.at[r, 8:128, :]))
    return [pltpu.make_async_copy(a, b, semaphore.at[k]) for k, (a, b) in enumerate(parts)]


def mask_kernel(rows, cols, counts, codes, state, *refs):
    strips, (rows8, came, semaphore) = refs[:6], refs[6:]
    first = pltpu.make_async_copy(state.at[:, 0:8, :], rows8, came)
    first.start()
    copies = fill_strips(rows, cols, state, strips, semaphore)
    for copy in copies:
        copy.start()
    first.wait()
    put_strips(rows, cols, codes, lambda r, c: live_rows(rows8[r * cols + c], counts[r, c]), strips)
    for copy in copies:
        copy.wait()


def mask_strips(rows, cols, counts, codes, state):
    return pl.pallas_call(
        functools.partial(mask_kernel, rows, cols),
        out_shape=strip_shapes(rows, cols),
        in_specs=[smem_spec(), smem_spec(), any_spec()],
        out_specs=(vmem_spec(),) * 6,
        scratch_shapes=[pltpu.VMEM((rows * cols, 8, 128), F32), pltpu.SemaphoreType.DMA(()), pltpu.SemaphoreType.DMA((6 + 2 * rows,))],
        compiler_params=FULL,
    )(counts, codes, state)


def linked(center, code, width):
    up = (code * 11) >> 5
    return center + up * (width - 3) + code - (width + 1)


def makers(rows, cols, row_t, row_s, side_t, side_s, mass, root, rho, squares):
    width = cols + 4
    row_mid, col_mid = (rows + 3) / 2.0, (cols + 3) / 2.0

    def geometry(flat, row, stride, n, index, apart, r, c, center, limit=None):
        def field(k):
            return flat[pl.ds(row + k, n, stride=stride), :]

        x = [field(0) + (r - row_mid), field(1) + (c - col_mid), field(2)]
        norm = x[0] * x[0] + x[1] * x[1] + x[2] * x[2]
        m = field(6)
        if limit is not None:
            m = jnp.where(lax.broadcasted_iota(I32, (n, 128), 1) < limit, m, 0.0)
        cube = jnp.exp2(jnp.log2(jnp.maximum(m, 1e-30)) * (1.0 / 3.0))
        cube = cube - (cube - m / (cube * cube)) * (1.0 / 3.0)
        cube = jnp.where(m > 0.0, cube, 0.0)

        def put(target, k, value):
            target[pl.ds(index * ROWS_K + k, n, stride=apart * ROWS_K), :] = value

        for k, value in enumerate([x[0] * cube, x[1] * cube, x[2] * cube, -norm * cube, cube]):
            hi, mid, low = thirds(value)
            for block, piece in enumerate((hi, mid, low, hi, mid, hi)):
                put(row_t, 5 * block + k, piece)
        put(row_t, 30, jnp.zeros_like(m))
        put(row_t, 31, jnp.zeros_like(m))
        for k in range(n):
            mass[pl.ds(index + k * apart, 1), :] = m[k : k + 1]
            root[pl.ds(index + k * apart, 1), :] = cube[k : k + 1]
        if center:
            for k, value in enumerate([x[0] + x[0], x[1] + x[1], x[2] + x[2], jnp.ones_like(m), 1.0 - norm]):
                hi, mid, low = thirds(value)
                for block, piece in enumerate((hi, hi, hi, mid, mid, low)):
                    put(row_s, 5 * block + k, piece)
            put(row_s, 30, jnp.zeros_like(m))
            put(row_s, 31, jnp.zeros_like(m))

    def sub(n):
        return sub_iota((n, 128)).astype(F32)

    quarter = lax.broadcasted_iota(I32, (128, 128), 1) // ROWS_K
    only = [jnp.where(quarter == k, 1.0, 0.0).astype(BF16) for k in range(4)]

    def block32(ref, index):
        return ref[pl.ds(pl.multiple_of(index * ROWS_K, ROWS_K), ROWS_K), :]

    def turn(indices):
        t = jnp.transpose(jnp.concatenate([block32(row_t, index) for index in indices], axis=0)).astype(BF16)
        for k, index in enumerate(indices):
            side_t[index] = t * only[k]
            side_s[index] = block32(row_s, index).astype(BF16)

    def density(center, partners, n):
        rhs = jnp.concatenate([side_s[center]] * 4, axis=0)
        total = jnp.zeros((8, 128), F32)
        for j, partner in enumerate(partners):
            y = jnp.maximum(jnp.dot(side_t[partner], rhs, preferred_element_type=F32), 0.0)
            square = y * y
            total = total + jnp.sum((square * y).reshape(16, 8, 128), axis=0)
            if n is not None:
                squares[n, j * 128 : (j + 1) * 128, :] = square.astype(BF16)
        rho[pl.ds(center, 1), :] = jnp.sum(total, axis=0, keepdims=True)

    return geometry, sub, turn, density


def own_copies(rows, cols, pairs, semaphore):
    width = cols + 4
    copies = []
    for source, target in pairs:
        for r in range(rows):
            part = pl.ds((r + 2) * width + 2, cols)
            copies.append(pltpu.make_async_copy(source.at[part], target.at[part], semaphore.at[len(copies)]))
    return copies


def inner_copies(rows, cols, source, target, semaphore):
    parts = [pl.ds(r * cols + 1, cols - 2) for r in range(1, rows - 1)]
    return [pltpu.make_async_copy(source.at[part], target.at[part], semaphore.at[k]) for k, part in enumerate(parts)]


def own_kernel(rows, cols, masked, *refs):
    if masked:
        counts, refs = refs[0], refs[1:]
    codes, cells_in, side_t_out, side_s_out, squares_out, mass, root, rho = refs[:8]
    geo, side_t, side_s, squares, row_t, row_s, geo_came, sides_left, squares_left = refs[8:]
    width = cols + 4
    own = rows * cols
    per = 8
    geometry, sub, turn, density = makers(rows, cols, row_t, row_s, side_t, side_s, mass, root, rho, squares)
    geo_copy = pltpu.make_async_copy(cells_in.at[:, 0:8, :], geo, geo_came)
    geo_copy.start()
    for ref in (mass, root, rho):
        ref[...] = jnp.ones_like(ref)
    geo_copy.wait()
    geo_flat = geo.reshape(own * 8, 128)

    def local_geo(i):
        first = i * per
        r, c = first // cols + 2, first % cols + 2
        limit = None
        if masked:
            limit = jnp.zeros((per, 128), I32)
            for k in range(per):
                limit = jnp.where(sub_iota((per, 128)) == k, counts[first // cols, first % cols + k], limit)
        geometry(geo_flat, first * 8, 8, per, r * width + c, 1, r.astype(F32), c.astype(F32) + sub(per), True, limit)

    loop(own // per, local_geo)
    def turn_own(i):
        for k in range(cols // 4):
            index = (i + 2) * width + 2 + 4 * k
            turn([index, index + 1, index + 2, index + 3])

    loop(rows, turn_own)

    sides = own_copies(rows, cols, ((side_t, side_t_out), (side_s, side_s_out)), sides_left)
    for copy in sides:
        copy.start()

    def inner_density(i):
        r = i + 1
        for k in range(1, cols - 1):
            center = (r + 2) * width + k + 2
            density(center, [linked(center, codes[j, r, k], width) for j in range(6)], r * cols + k)

    loop(rows - 2, inner_density)
    inner = inner_copies(rows, cols, squares, squares_out, squares_left)
    for copy in inner:
        copy.start()
    for copy in sides + inner:
        copy.wait()


def own_call(rows, cols, counts, codes, cells):
    own = rows * cols
    patch = (rows + 4) * (cols + 4)
    scalars = [] if counts is None else [counts]
    field = jax.ShapeDtypeStruct((patch, 128), F32)
    return pl.pallas_call(
        functools.partial(own_kernel, rows, cols, counts is not None),
        out_shape=(jax.ShapeDtypeStruct((patch, 128, 128), BF16), jax.ShapeDtypeStruct((patch, 32, 128), BF16), jax.ShapeDtypeStruct((own, 768, 128), BF16), field, field, field),
        in_specs=[smem_spec()] * (len(scalars) + 1) + [any_spec()],
        out_specs=(any_spec(),) * 3 + (vmem_spec(),) * 3,
        scratch_shapes=[
            pltpu.VMEM((own, 8, 128), F32),
            pltpu.VMEM((patch, 128, 128), BF16),
            pltpu.VMEM((patch, 32, 128), BF16),
            pltpu.VMEM((own, 768, 128), BF16),
            pltpu.VMEM((patch * ROWS_K, 128), F32),
            pltpu.VMEM((patch * ROWS_K, 128), F32),
            pltpu.SemaphoreType.DMA(()),
            pltpu.SemaphoreType.DMA((2 * rows,)),
            pltpu.SemaphoreType.DMA((rows - 2,)),
        ],
        compiler_params=pltpu.CompilerParams(vmem_limit_bytes=50 * MIB),
        cost_estimate=pl.CostEstimate(flops=5 * 10**9, bytes_accessed=16 * MIB, transcendentals=0),
    )(*scalars, codes, cells)


def step_kernel(rows, cols, masked, leaving, ahead, *refs):
    if masked:
        counts, refs = refs[0], refs[1:]
    codes, segments, contact, cells_in, a_low, a_high, z_low, z_high = refs[:8]
    if ahead:
        side_t_in, side_s_in, squares_in, mass_in, root_in, rho_in = refs[8:14]
        refs = refs[:8] + refs[14:]
    if leaving:
        slots, buffer_row, out_ref, sent, gathered = refs[8:13]
        refs = refs[13:]
    else:
        out_ref, dens = refs[8:10]
        refs = refs[10:]
    geo, cells, out, side_t, side_s, feat, squares, row_t, row_s = refs[:9]
    mass, root, rho, ratio, inverse, ring_codes, geo_came, sides_came, squares_came, cells_came, out_left, codes_came = refs[9:]
    width = cols + 4
    own = rows * cols
    z_rows = rows * EDGE
    per_device = segments.shape[1] // 3
    sub8 = sub_iota((8, 128))
    row_mid, col_mid = (rows + 3) / 2.0, (cols + 3) / 2.0

    if not ahead:
        geo_copy = pltpu.make_async_copy(cells_in.at[:, 0:8, :], geo, geo_came)
        geo_copy.start()
    code_copies = []

    def bring_codes(source, first, n):
        code_copies.append(pltpu.make_async_copy(source, ring_codes.at[pl.ds(first, n), :], codes_came.at[len(code_copies)]))

    bring_codes(a_low.at[:, EDGE - 1, :], 0, cols)
    bring_codes(a_high.at[:, EDGE - 1, :], cols, cols)
    for ref, first in ((z_low, 2 * cols), (z_high, 2 * cols + rows + 2)):
        for r in range(rows):
            bring_codes(ref.at[pl.ds(r * EDGE + EDGE - 1, 1), :], first + r, 1)
        for n in range(2):
            bring_codes(ref.at[pl.ds(z_rows + n * CORNER + EDGE - 1, 1), :], first + rows + n, 1)
    cells_piece = pieces(cells_in, cells, cells_came, 8)
    out_piece = pieces(out, out_ref, out_left, 8)
    for copy in code_copies:
        copy.start()
    for i in range(own // 8):
        cells_piece(i).start()

    geometry, sub, turn, density = makers(rows, cols, row_t, row_s, side_t, side_s, mass, root, rho, squares)
    per = 8
    if ahead:
        for copy in own_copies(rows, cols, ((side_t_in, side_t), (side_s_in, side_s)), sides_came) + inner_copies(rows, cols, squares_in, squares, squares_came):
            copy.start()
        for source, target in ((mass_in, mass), (root_in, root), (rho_in, rho)):
            target[...] = source[...]
    else:
        rho[...] = jnp.ones_like(rho)
        geo_copy.wait()
    geo_flat = geo.reshape(own * 8, 128)

    def local_geo(i):
        first = i * per
        r, c = first // cols + 2, first % cols + 2
        limit = None
        if masked:
            limit = jnp.zeros((per, 128), I32)
            for k in range(per):
                limit = jnp.where(sub_iota((per, 128)) == k, counts[first // cols, first % cols + k], limit)
        geometry(geo_flat, first * 8, 8, per, r * width + c, 1, r.astype(F32), c.astype(F32) + sub(per), True, limit)

    if not ahead:
        loop(own // per, local_geo)
    for ref, first, second in ((a_low, 1, 0), (a_high, rows + 2, rows + 3)):
        flat = ref.reshape(cols * EDGE, 128)
        for k in range(0, cols, per):
            c = k + 2.0 + sub(per)
            geometry(flat, k * EDGE, EDGE, per, first * width + k + 2, 1, float(first), c, True)
            geometry(flat, k * EDGE + 128, EDGE, per, second * width + k + 2, 1, float(second), c, False)
    for ref, near, far in ((z_low, 1, 0), (z_high, cols + 2, cols + 3)):
        r = 2.0 + sub(rows)
        geometry(ref, 0, EDGE, rows, 2 * width + near, width, r, float(near), True)
        geometry(ref, 128, EDGE, rows, 2 * width + far, width, r, float(far), False)
        apart = (rows + 1) * width
        r = 1.0 + (rows + 1.0) * sub(2)
        geometry(ref, z_rows, CORNER, 2, width + near, apart, r, float(near), True)
        geometry(ref, z_rows + 136, CORNER, 2, width + far, apart, r, float(far), False)
        apart = (rows + 3) * width
        r = (rows + 3.0) * sub(2)
        geometry(ref, z_rows + 128, CORNER, 2, near, apart, r, float(near), False)
        geometry(ref, z_rows + 144, CORNER, 2, far, apart, r, float(far), False)

    def turn_own(i):
        for k in range(cols // 4):
            index = (i + 2) * width + 2 + 4 * k
            turn([index, index + 1, index + 2, index + 3])

    if not ahead:
        loop(rows, turn_own)

    def turn_ring(i):
        for r in (i, i + rows + 2):
            for k in range(width // 4):
                index = r * width + 4 * k
                turn([index, index + 1, index + 2, index + 3])
        for r in (2 * i + 2, 2 * i + 3):
            turn([r * width, r * width + 1, r * width + cols + 2, r * width + cols + 3])

    loop(2, turn_ring)

    def own_cell(r, c):
        center = (r + 2) * width + c + 2
        density(center, [linked(center, codes[j, r, c], width) for j in range(6)], r * cols + c)

    def whole_row(r):
        for c in range(cols):
            own_cell(r, c)

    if ahead:
        for copy in own_copies(rows, cols, ((side_t_in, side_t), (side_s_in, side_s)), sides_came):
            copy.wait()
        loop(2, lambda i: whole_row(i * (rows - 1)))
        for r in range(1, rows - 1):
            own_cell(r, 0)
            own_cell(r, cols - 1)
    else:
        loop(rows, whole_row)
    for copy in code_copies:
        copy.wait()

    def ring_cell(center, n):
        density(center, [linked(center, ring_codes[n, j].astype(I32), width) for j in range(6)], None)

    def ring_rows(i):
        for k in range(8):
            c = i * 8 + k
            ring_cell(width + c + 2, c)
            ring_cell((rows + 2) * width + c + 2, cols + c)

    loop(cols // 8, ring_rows)
    for k, r in enumerate([r + 2 for r in range(rows)] + [1, rows + 2]):
        ring_cell(r * width + 1, 2 * cols + k)
        ring_cell(r * width + cols + 2, 2 * cols + rows + 2 + k)

    living = mass[...] > 0.0
    guarded = jnp.where(living, rho[...], 1.0)
    ratio[...] = jnp.where(living, (guarded - 1.0) / (guarded * guarded), 0.0)
    inverse[...] = jnp.where(living, 1.0 / guarded, 0.0)

    def row8(ref, index):
        return rows_of(ref[pl.ds(index, 1), :], 8)

    def shifted(g, r, c):
        off_r = r.astype(F32) - row_mid
        off_c = c.astype(F32) - col_mid
        return jnp.where(sub8 == 0, g + off_r, jnp.where(sub8 == 1, g + off_c, g))

    def positions(g, r, c):
        x = shifted(g, r, c)
        return jnp.where((sub8 == 0) | (sub8 == 4), 1.0, jnp.where(sub8 < 4, pltpu.roll(x, 1, 0), pltpu.roll(x, 5, 0)))

    def features(load, r, c):
        index = r * width + c
        cube = row8(root, index)
        scale = cube * row8(inverse, index)

        g = load(0)
        nu = rows_of(g[7:8], 8)
        first = jnp.where(sub8 < 3, pltpu.roll(g, 5, 0) * nu, jnp.where(sub8 == 6, 1.0, g)) * scale
        press = positions(g, r, c) * jnp.where(sub8 < 4, cube, cube * row8(ratio, index))
        hi, lo = halves(press)
        feat[index, 128:144, :] = jnp.concatenate([hi.astype(F32), lo.astype(F32)], axis=0).astype(BF16)
        feat[index, 0:16, :] = jnp.concatenate([first, load(1) * scale], axis=0).astype(BF16)
        for k in range(1, 8):
            feat[index, 16 * k : 16 * k + 16, :] = jnp.concatenate([load(2 * k) * scale, load(2 * k + 1) * scale], axis=0).astype(BF16)

    def in_cell(ref, n):
        return lambda k: ref[n, 8 * k : 8 * k + 8, :]

    def in_rows(ref, row):
        return lambda k: ref[row + 8 * k : row + 8 * k + 8, :]

    def local_feat(i):
        cells_piece(i).wait()
        for k in range(8):
            n = i * 8 + k
            features(in_cell(cells, n), n // cols + 2, n % cols + 2)

    if ahead:
        for copy in inner_copies(rows, cols, squares_in, squares, squares_came):
            copy.wait()
    loop(own // 8, local_feat)

    def a_feat(i):
        for k in range(4):
            n = i * 4 + k
            features(in_cell(a_low, n), jnp.int32(1), n + 2)
            features(in_cell(a_high, n), jnp.int32(rows + 2), n + 2)

    loop(cols // 4, a_feat)
    for ref, c in ((z_low, 1), (z_high, cols + 2)):
        for r in range(rows):
            features(in_rows(ref, r * EDGE), jnp.int32(r + 2), jnp.int32(c))
        for n, r in enumerate((1, rows + 2)):
            features(in_rows(ref, z_rows + n * CORNER), jnp.int32(r), jnp.int32(c))

    def force(n):
        r, c = n // cols, n % cols
        index = (r + 2) * width + c + 2
        lhs = jnp.concatenate([feat[linked(index, codes[j, r, c], width)] for j in range(6)], axis=1)
        sums = jnp.dot(lhs, squares[n], preferred_element_type=F32)
        if masked:
            held = lax.broadcasted_iota(I32, (8, 128), 1) < counts[r, c]

        def load(k):
            value = cells[n, 8 * k : 8 * k + 8, :]
            return jnp.where(held, value, 0.0) if masked else value

        g = load(0)
        m, nu = rows_of(g[6:7], 8), rows_of(g[7:8], 8)
        alive = jnp.where(m > 0.0, time_step, 0.0)
        first = sums[0:8]
        press = sums[128:136] + sums[136:144]
        press = press - positions(g, r + 2, c + 2) * jnp.where(sub8 < 4, rows_of(press[0:1], 8), rows_of(press[4:5], 8))
        press = press * jnp.where(sub8 < 4, row8(ratio, index), 1.0)
        press = press + pltpu.roll(press, 4, 0)
        weight, friction = rows_of(first[6:7], 8), rows_of(first[7:8], 8)
        touching = contact[r, c]
        device, place = touching // per_device, (touching % per_device) * 3
        surface = jnp.where(sub8 == 3, segments[device, place], jnp.where(sub8 == 4, segments[device, place + 1], segments[device, place + 2]))
        wall = wall_gain * jnp.maximum(1.0 - 3.0 * rows_of(g[2:3], 8), 0.0)
        accel = nu * (first - g * weight) + pltpu.roll(first, 3, 0) - g * friction + wall * (surface - g)
        accel = accel - 6.0 * pltpu.roll(press, 2, 0)
        velocity = g + accel * alive
        position = g + time_step * pltpu.roll(velocity, 5, 0)
        out[n, 0:8, :] = jnp.where(sub8 < 3, position, jnp.where(sub8 < 6, velocity, g))
        gain = 2.0 * alive
        stay = 1.0 - gain * weight
        for k in range(1, 16):
            out[n, 8 * k : 8 * k + 8, :] = load(k) * stay + gain * sums[8 * k : 8 * k + 8]
        if not leaving:
            dens[pl.ds(n, 1), :] = jnp.where(m > 0.0, row8(rho, index), 0.0)[0:1]

    def forces(i):
        for k in range(8):
            force(i * 8 + k)
        if not leaving:
            out_piece(i).start()

    loop(own // 8, forces)
    if leaving:
        take_out(out, slots, buffer_row, sent, gathered, out_piece)
    for i in range(own // 8):
        out_piece(i).wait()


def take_out(state, slots, buffer_row, sent, gathered, out_piece):
    leaving, places = slots.shape[0], sent.shape[0]
    offset = jnp.broadcast_to(slots[...], (leaving, 128)) - lax.broadcasted_iota(I32, (leaving, 128), 1)
    gathered[...] = jnp.zeros_like(gathered)
    per = 8

    def body(i):
        hits, parts = [], []
        for k in range(per):
            c = i * per + k
            hit = jnp.where(offset == c * 128, 1.0, 0.0)
            gone = jnp.sum(hit, axis=0, keepdims=True)
            whole = state[c]
            hi, lo = halves(whole)
            hits.append(hit.astype(BF16))
            parts.append(jnp.concatenate([hi, lo], axis=0))
            state[c] = whole * (1.0 - gone)
        gathered[...] += lax.dot_general(jnp.concatenate(hits, axis=1), jnp.concatenate(parts, axis=1), (((1,), (1,)), ((), ())), preferred_element_type=F32)
        out_piece(i).start()

    loop(state.shape[0] // per, body)
    place = jnp.where(jnp.broadcast_to(buffer_row[...], (places, leaving)) == sub_iota((places, leaving)), 1.0, 0.0).astype(BF16)
    right = jnp.concatenate([gathered[...].astype(BF16), jnp.ones((leaving, 128), BF16)], axis=1)
    sums = jnp.dot(place, right, preferred_element_type=F32)
    lane = lax.broadcasted_iota(I32, (places, 128), 1)
    sent[...] = jnp.where((lane == 6) & (sums[:, 256:384] < 0.5), -1.0, sums[:, 0:128] + sums[:, 128:256])


def smem_spec():
    return pl.BlockSpec(memory_space=pltpu.SMEM)


def vmem_spec():
    return pl.BlockSpec(memory_space=pltpu.VMEM)


def step_call(rows, cols, counts, codes, segments, contact, cells, halo, ahead, leave=None):
    own = rows * cols
    patch = (rows + 4) * (cols + 4)
    ring = 2 * cols + 2 * (rows + 2)
    new = jax.ShapeDtypeStruct((own, 128, 128), F32)
    extra, first = [], []
    if leave:
        slots, buffer_row, places = leave
        outs = (new, jax.ShapeDtypeStruct((places, 128), F32))
        extra, first = [slots, buffer_row], [pltpu.VMEM((slots.shape[0], 256), F32)]
    else:
        outs = (new, jax.ShapeDtypeStruct((own, 128), F32))
    scalars = [] if counts is None else [counts]
    return pl.pallas_call(
        functools.partial(step_kernel, rows, cols, counts is not None, bool(leave), ahead is not None),
        out_shape=outs,
        in_specs=[smem_spec()] * (len(scalars) + 3) + [any_spec()] + [vmem_spec()] * 4 + ([] if ahead is None else [any_spec()] * 3 + [vmem_spec()] * 3) + [vmem_spec()] * len(extra),
        out_specs=(any_spec(), vmem_spec()),
        scratch_shapes=first
        + [
            pltpu.VMEM((own, 8, 128), F32),
            pltpu.VMEM((own, 128, 128), F32),
            pltpu.VMEM((own, 128, 128), F32),
            pltpu.VMEM((patch, 128, 128), BF16),
            pltpu.VMEM((patch, 32, 128), BF16),
            pltpu.VMEM((patch, 144, 128), BF16),
            pltpu.VMEM((own, 768, 128), BF16),
            pltpu.VMEM((patch * ROWS_K, 128), F32),
            pltpu.VMEM((patch * ROWS_K, 128), F32),
        ]
        + [pltpu.VMEM((patch, 128), F32)] * 5
        + [
            pltpu.SMEM((ring, 128), F32),
            pltpu.SemaphoreType.DMA(()),
            pltpu.SemaphoreType.DMA((2 * rows,)),
            pltpu.SemaphoreType.DMA((rows - 2,)),
            pltpu.SemaphoreType.DMA((own // 8,)),
            pltpu.SemaphoreType.DMA((own // 8,)),
            pltpu.SemaphoreType.DMA((2 + 2 * (rows + 2),)),
        ],
        compiler_params=pltpu.CompilerParams(vmem_limit_bytes=47 * MIB),
    )(*scalars, codes, segments, contact, cells, *halo, *(ahead or ()), *extra)


def insert_kernel(rows, cols, codes, state_in, incoming, slots, out_ref, *refs):
    strips, (state, out, came, left_for, semaphore) = refs[:6], refs[6:]
    arrive = pieces(state_in, state, came, 8)
    leave = pieces(out, out_ref, left_for, 8)
    for i in range(rows * cols // 8):
        arrive(i).start()
    places = slots.shape[0]
    data = incoming[...]
    absent = jnp.broadcast_to(data[:, 6:7], (places, 128)) < 0.0
    offset = jnp.broadcast_to(slots[...], (places, 128)) - lax.broadcasted_iota(I32, (places, 128), 1)
    offset = jnp.where(absent, -1, offset)
    hi, lo = halves(jnp.transpose(data))
    left = jnp.concatenate([hi, lo, jnp.ones((16, places), BF16)], axis=0)
    per = 8

    def body(i):
        arrive(i).wait()
        for pair in range(per // 2):
            first = i * per + pair * 2
            hits = [jnp.where(offset == (first + k) * 128, 1.0, 0.0).astype(BF16) for k in range(2)]
            sums = jnp.dot(left, jnp.concatenate(hits, axis=1), preferred_element_type=F32)
            for k in range(2):
                part = sums[:, 128 * k : 128 * (k + 1)]
                out[first + k] = state[first + k] * (1.0 - part[256:257]) + (part[0:128] + part[128:256])
        leave(i).start()

    loop(rows * cols // per, body)
    copies = fill_strips(rows, cols, out, strips, semaphore)
    for copy in copies:
        copy.start()
    put_strips(rows, cols, codes, lambda r, c: out[r * cols + c, 0:8, :], strips)
    for copy in copies:
        copy.wait()
    for i in range(rows * cols // per):
        leave(i).wait()


def insert(rows, cols, codes, state, incoming, slots):
    own = rows * cols
    return pl.pallas_call(
        functools.partial(insert_kernel, rows, cols),
        out_shape=(jax.ShapeDtypeStruct(state.shape, F32),) + strip_shapes(rows, cols),
        in_specs=[smem_spec(), any_spec(), vmem_spec(), vmem_spec()],
        out_specs=(any_spec(),) + (vmem_spec(),) * 6,
        scratch_shapes=[pltpu.VMEM((own, 128, 128), F32)] * 2 + [pltpu.SemaphoreType.DMA((own // 8,))] * 2 + [pltpu.SemaphoreType.DMA((6 + 2 * rows,))],
        compiler_params=pltpu.CompilerParams(vmem_limit_bytes=52 * MIB),
    )(codes, state, incoming, slots)


def swap(up, down, axis):
    n = lax.axis_size(axis)
    pairs = [(i, (i + 1) % n) for i in range(n if axis == "az" else n - 1)]
    return lax.ppermute(up, axis, pairs), lax.ppermute(down, axis, [(j, i) for i, j in pairs])


def exchange(strips):
    ends_up, ends_down, a_up, a_down, z_up, z_down = strips
    low, high = swap(ends_up, ends_down, "ax")
    a_low, a_high = swap(a_up, a_down, "ax")

    def beside(strip, n):
        return jnp.concatenate([strip.reshape(-1, 128), low[n], high[n]], axis=0)

    sides = beside(z_up, 1), beside(z_down, 0)
    return (a_low, a_high) + swap(*sides, "az"), sides


def local(particles, counts, pair_codes, contact, twist_state, leaving_slot, leaving_dest, arrival_slot):
    rows, cols, fields, block = particles.shape
    ranks = lax.axis_size("ax") * lax.axis_size("az")
    own = rows * cols
    state = particles.reshape(own, fields, block)
    pair_codes = pair_codes.transpose(2, 0, 1)
    halo, sides = exchange(mask_strips(rows, cols, counts, pair_codes, state))

    segments = twist_state.shape[0]
    twist_state, _ = lax.optimization_barrier((twist_state, sides))
    told = jnp.broadcast_to(twist_state.reshape(1, segments * 3), (ranks, segments * 3))
    told = lax.all_to_all(told, AXES, 0, 0, tiled=True)

    dest = leaving_dest[:, 0]
    leaving = dest.shape[0]
    same = dest[:, None] == dest[None, :]
    earlier = lax.broadcasted_iota(I32, (leaving, leaving), 0) > lax.broadcasted_iota(I32, (leaving, leaving), 1)
    order = jnp.sum((same & earlier).astype(I32), axis=1)
    capacity = arrival_slot.shape[0] // ranks
    buffer_row = (dest * capacity + order).reshape(1, leaving)

    leave = (leaving_slot.reshape(-1, 1), buffer_row, ranks * capacity)
    state, outgoing = step_call(rows, cols, counts, pair_codes, told, contact, state, halo, None, leave)
    incoming = lax.all_to_all(outgoing.reshape(ranks, capacity, fields), AXES, 0, 0, tiled=True)
    state, *strips = insert(rows, cols, pair_codes, state, incoming.reshape(-1, fields), arrival_slot.reshape(-1, 1))
    halo, sides = exchange(strips)
    ahead = own_call(rows, cols, None, pair_codes, lax.optimization_barrier((state, sides))[0])
    state, density = step_call(rows, cols, None, pair_codes, told, contact, state, halo, ahead)
    return state.reshape(particles.shape), density.reshape(rows, cols, block)


def solution(mesh):
    both = P("ax", "az")
    flat = P(AXES)
    return jax.shard_map(
        local,
        mesh=mesh,
        in_specs=(P("ax", "az", None, None), both, P("ax", "az", None), both, P(AXES, None), flat, P(AXES, None), flat),
        out_specs=(P("ax", "az", None, None), P("ax", "az", None)),
        check_vma=False,
    )
```
